512 devices in a mesh: outer: 32 (over z, core), inner: 16 (over x, y).
Axes of the slice: x: 4, y: 4, z: 16, core: 2. Of those that a mesh axis runs over, the one named last changes fastest.
Arguments:
- queries: bfloat16 [196608, 1536], P(('outer', 'inner')), may hold values from -6 to 6
- key_vectors: bfloat16 [196608, 1536], P(('outer', 'inner')), may hold values from -6 to 6
- value_vectors: bfloat16 [196608, 1536], P(('outer', 'inner')), may hold values from -6 to 6
- write_gate: float32 [12, 196608], P(None, ('outer', 'inner')), may hold values from 0.05 to 1
- ridge_term: float32 [12], replicated, may hold values from 0.25 to 4
- segment_ids: int32 [196608], P(('outer', 'inner')), may hold values from 0 to 255, never falling along the last dimension, each value on 1 to 1536 neighbouring positions
Outputs:
- mixed_heads: bfloat16 [196608, 1536], P(('outer', 'inner'))
The draws below stay inside these ranges and needn't reach their ends.
Inputs may be any that keep to these rules, and one draw needn't show every extreme that they name: `segment_ids`: segment ids never fall along the tokens; each of the 256 documents spans 1 to 1536 tokens, one exactly 1536.
All inputs are finite; a program needn't handle non-finite values.
Results may differ from the reference program's by a relative error of at most 0.001.
Values sent between devices are 32-bit elements; how exact they have to be, the bound alone decides.
No kernel may reach another device: no remote copies, remote signals or barrier semaphores. Data moves between devices by JAX's collectives and lax.ppermute only.
A program may use at most 64 MiB of HBM per device.

```python
import math
import jax
import jax.numpy as jnp
import numpy as np
from jax import lax

HEADS = 12
DH = 128
STRETCH = 128
ITERS = 4
TOKENS = 196608
DOC_MOST = 1536
DOCS = 256


def level_of(rng, extent, pieces, least, largest):
    def one(axis_at, shards_of):
        draws = jax.random.uniform(jax.random.fold_in(jax.random.fold_in(rng, 6), axis_at), (shards_of,), jnp.float32, least / len(pieces), largest / len(pieces))
        return jnp.repeat(jnp.exp(draws), extent[axis_at] // shards_of).reshape((-1,) + (1,) * (len(extent) - axis_at - 1))

    factor_of = one(*pieces[0])
    for cut in pieces[1:]:
        factor_of = factor_of * one(*cut)
    return factor_of


def profile(count, total, reach, lean):
    loads = [(1 << 20) // math.isqrt(rank ** lean) + 1 for rank in range(2, count + 1)]
    spare, given = total - reach - (count - 1), [1] * (count - 1)
    while spare > 0:
        candidates = [i for i in range(count - 1) if given[i] < reach]
        pool, left = sum([loads[i] for i in candidates]), spare
        for i in candidates:
            more = min(reach - given[i], max(1, left * loads[i] // pool), spare)
            given[i] = given[i] + more
            spare = spare - more
    return np.array([reach] + given)


def uneven(own_key, amount, total, bound, skew):
    if amount == 2:
        one = jax.random.randint(own_key, (), max(1, total - bound), min(bound, total - 1) + 1)
        return jnp.stack([one, total - one])
    sizes = jnp.asarray(profile(amount, total, bound, skew), jnp.int32)
    pairs = (amount - 1) // 2
    giver, taker = sizes[1:1 + 2 * pairs:2], sizes[2:2 + 2 * pairs:2]
    slack = jnp.minimum(giver - 1, bound - taker)
    passed = jax.random.randint(jax.random.fold_in(own_key, 1), (pairs,), 0, 1 << 20) % (slack + 1)
    sizes = sizes.at[1:1 + 2 * pairs:2].set(giver - passed).at[2:2 + 2 * pairs:2].set(taker + passed)
    return sizes[jax.random.permutation(jax.random.fold_in(own_key, 2), amount)]


def centred(rng, dims, scale, limit, split=(), dtype=jnp.bfloat16):
    drawn = scale * jax.random.normal(rng, dims, jnp.float32)
    if split:
        drawn = drawn * level_of(rng, dims, split, -0.22, 0.18)
    return jnp.clip(drawn, -limit, limit).astype(dtype)


def setup_inputs(seed: int = 0) -> dict:
    splits = jax.random.split(jax.random.key(seed), 7)
    queries = centred(splits[0], (TOKENS, HEADS * DH), 1.0, 6.0, ((0, 512),))
    key_vectors = centred(splits[1], (TOKENS, HEADS * DH), 1.0, 6.0, ((0, 512),))
    value_vectors = centred(splits[2], (TOKENS, HEADS * DH), 1.0, 6.0, ((0, 512),))
    write_gate = jnp.clip(jnp.exp(math.log(1.0) - 2.9957323 * jax.random.uniform(splits[3], (HEADS, TOKENS), jnp.float32) ** level_of(splits[3], (HEADS, TOKENS), ((1, 512),), -0.2, 0.2)), 0.05, 1.0)
    ridge_term = jnp.clip(jnp.exp(jax.random.uniform(splits[4], (HEADS,), jnp.float32, math.log(0.25), math.log(4.0))), 0.25, 4.0)
    segment_ids = jnp.searchsorted(jnp.cumsum(uneven(splits[5], DOCS, TOKENS, DOC_MOST, 2)), jnp.arange(TOKENS), side="right").astype(jnp.int32)
    return {"queries": queries, "key_vectors": key_vectors, "value_vectors": value_vectors, "write_gate": write_gate, "ridge_term": ridge_term, "segment_ids": segment_ids}


highest = lax.Precision.HIGHEST

def normed_heads(raw, heads):
    rows = raw.shape[0]
    values = raw.astype(jnp.float32).reshape(rows, heads, -1).transpose(1, 0, 2)
    return values * lax.rsqrt(lax.optimization_barrier(jnp.sum(values * values, axis=-1, keepdims=True)) + 1e-06)

def block_step(carry, block, ridge_term):
    gram, memory, previous = carry
    query_raw, key_raw, value_raw, gate_rows, seg_rows = block
    heads = ridge_term.shape[0]
    query_rows = normed_heads(query_raw, heads)
    key_rows = normed_heads(key_raw, heads)
    value_rows = value_raw.astype(jnp.float32).reshape(value_raw.shape[0], heads, -1).transpose(1, 0, 2)
    length = seg_rows.shape[0]
    keep = (seg_rows == previous).astype(jnp.float32)[None, :, None]
    order = jnp.arange(length)
    causal = (seg_rows[:, None] == seg_rows[None, :]) & (order[None, :] <= order[:, None])
    weights = causal.astype(jnp.float32)[None] * gate_rows[:, None, :]

    def apply_gram(direction):
        carried = jnp.einsum('hte,hed->htd', direction, gram, precision=highest) * keep
        scores = jnp.einsum('htd,hsd->hts', direction, key_rows, precision=highest) * weights
        inside = jnp.einsum('hts,hsd->htd', scores, key_rows, precision=highest)
        return carried + inside + ridge_term[:, None, None] * direction
    solved = jnp.zeros_like(query_rows)
    residual = query_rows
    direction = query_rows
    resid_sq = lax.optimization_barrier(jnp.sum(residual * residual, axis=-1, keepdims=True))
    for sweep in range(ITERS):
        image = apply_gram(direction)
        step_size = resid_sq / lax.optimization_barrier(jnp.sum(direction * image, axis=-1, keepdims=True))
        solved = solved + step_size * direction
        residual = residual - step_size * image
        fresh_sq = lax.optimization_barrier(jnp.sum(residual * residual, axis=-1, keepdims=True))
        direction = residual + fresh_sq / resid_sq * direction
        resid_sq = fresh_sq
    carried_out = jnp.einsum('htk,hvk->htv', solved, memory, precision=highest) * keep
    scores = jnp.einsum('htd,hsd->hts', solved, key_rows, precision=highest) * weights
    inside_out = jnp.einsum('hts,hsv->htv', scores, value_rows, precision=highest)
    result = (carried_out + inside_out).transpose(1, 0, 2).reshape(length, -1).astype(jnp.bfloat16)
    last_id = seg_rows[length - 1]
    stay = (last_id == previous).astype(jnp.float32)
    tail = (seg_rows == last_id).astype(jnp.float32)[None, :] * gate_rows
    key_tail = key_rows * tail[:, :, None]
    gram_next = stay * gram + jnp.einsum('hsk,hsl->hkl', key_tail, key_rows, precision=highest)
    memory_next = stay * memory + jnp.einsum('hsv,hsk->hvk', value_rows * tail[:, :, None], key_rows, precision=highest)
    return ((gram_next, memory_next, last_id), result)

def reference(queries, key_vectors, value_vectors, write_gate, ridge_term, segment_ids):
    blocks = TOKENS // STRETCH
    width = queries.shape[1]
    heads = ridge_term.shape[0]
    head_size = width // heads
    gate_blocks = write_gate.reshape(heads, blocks, STRETCH).transpose(1, 0, 2)
    xs = (queries.reshape(blocks, STRETCH, width), key_vectors.reshape(blocks, STRETCH, width), value_vectors.reshape(blocks, STRETCH, width), gate_blocks, segment_ids.reshape(blocks, STRETCH))
    zeros = jnp.zeros((heads, head_size, head_size), jnp.float32)
    init = (zeros, zeros, segment_ids[0])
    final, outputs = lax.scan(lambda carry, block: block_step(carry, block, ridge_term), init, xs)
    return outputs.reshape(TOKENS, width)
```

```python
import jax
import jax.numpy as jnp
from jax import lax
from jax.experimental import pallas as pl
from jax.experimental.pallas import tpu as pltpu
from jax.sharding import PartitionSpec as P

STRETCH = 128
ITERS = 4
REACH = 4
AXES = ("outer", "inner")
VMEM_LIMIT = 56 * 1024 * 1024


def halves(x):
    high = x.astype(jnp.bfloat16)
    return high, (x - high.astype(jnp.float32)).astype(jnp.bfloat16)


def twice(x, axis):
    return jnp.concatenate([x, x], axis=axis)


def wide(x):
    return jnp.concatenate(halves(x), axis=1)


def dot_nt(a, b):
    return lax.dot_general(a, b, (((1,), (1,)), ((), ())), preferred_element_type=jnp.float32)


def dot_nn(a, b):
    return lax.dot_general(a, b, (((1,), (0,)), ((), ())), preferred_element_type=jnp.float32)


def same(a, b):
    return (a == b).astype(jnp.float32)


def state_kernel(ids, key_ref, value_ref, gate_ref, segs_ref, gram_ref, memory_ref, grams_ref, memories_ref, wg_ref, wm_ref):
    head = pl.program_id(0)
    tokens = key_ref.shape[0]
    blocks = tokens // STRETCH
    keys = key_ref[...]
    keys_t = keys.astype(jnp.float32).T
    values_t = value_ref[...].astype(jnp.float32).T
    scale = lax.rsqrt(jnp.sum(keys_t * keys_t, axis=0, keepdims=True) + 1e-06)
    for_memory = gate_ref[pl.ds(head, 1), :] * scale
    for_gram = for_memory * scale
    wg_ref[pl.ds(head, 1), :] = for_gram
    wm_ref[pl.ds(head, 1), :] = for_memory
    gram = memory = None
    for b in range(blocks):
        here = slice(b * STRETCH, (b + 1) * STRETCH)
        last = ids[(b + 1) * STRETCH - 1]
        tail = same(segs_ref[:, here], last)
        twin = twice(keys[here], 0)
        gram_here = dot_nn(wide(keys_t[:, here] * (for_gram[:, here] * tail)), twin)
        memory_here = dot_nn(wide(values_t[:, here] * (for_memory[:, here] * tail)), twin)
        if b:
            joined = same(last, ids[b * STRETCH - 1])
            gram_here = gram_here + joined * gram
            memory_here = memory_here + joined * memory
        gram, memory = gram_here, memory_here
        if b < blocks - 1:
            grams_ref[0, b] = gram
            memories_ref[0, b] = memory
    gram_ref[0] = gram
    memory_ref[0] = memory


def solve_kernel(ids, ridge, query_ref, key_ref, value_ref, seg_col_ref, segs_ref, wg_ref, wm_ref, in_gram_ref, grams_ref, memories_ref, solved_ref, partial_ref, mask_ref):
    head = pl.program_id(0)
    tokens = key_ref.shape[0]
    blocks = tokens // STRETCH

    @pl.when(head == 0)
    def _():
        order = lax.broadcasted_iota(jnp.int32, (STRETCH, STRETCH), 0)
        causal = order >= lax.broadcasted_iota(jnp.int32, (STRETCH, STRETCH), 1)
        for b in range(blocks):
            here = slice(b * STRETCH, (b + 1) * STRETCH)
            equal = seg_col_ref[here, :] == segs_ref[:, here]
            mask_ref[b] = jnp.where(causal & equal, 1.0, 0.0)

    lam = ridge[head]
    for_gram = wg_ref[pl.ds(head, 1), :]
    for_memory = wm_ref[pl.ds(head, 1), :]
    for b in range(blocks):
        here = slice(b * STRETCH, (b + 1) * STRETCH)
        previous = ids[max(b * STRETCH - 1, 0)]
        keep = same(seg_col_ref[here, :], previous)
        gram = in_gram_ref[0]
        if b:
            joined = same(previous, ids[0])
            gram = grams_ref[0, b - 1] + joined * gram
        gram_high, gram_low = halves(gram)
        keys = key_ref[here, :]
        pair = twice(keys, 1)
        twin = twice(keys, 0)
        right = jnp.concatenate([twice(gram_high, 1), twice(gram_low, 1), pair], axis=0)
        weights = mask_ref[b] * for_gram[:, here]
        query = query_ref[here, :].astype(jnp.float32)
        query = query * lax.rsqrt(jnp.sum(query * query, axis=1, keepdims=True) + 1e-06)
        residual = direction = query
        solved = None
        size_sq = jnp.sum(query * query, axis=1, keepdims=True)
        for sweep in range(ITERS):
            found = dot_nt(wide(direction), right)
            carried = (found[:, :STRETCH] + found[:, STRETCH:2 * STRETCH]) * keep + lam * direction
            scores = found[:, 2 * STRETCH:]
            weighed = scores * weights
            across = jnp.sum(weighed * scores + carried * direction, axis=1, keepdims=True)
            step = size_sq / across
            move = step * direction
            solved = move if solved is None else solved + move
            if sweep < ITERS - 1:
                image = carried + dot_nn(wide(weighed), twin)
                residual = residual - step * image
                fresh_sq = jnp.sum(residual * residual, axis=1, keepdims=True)
                direction = residual + (fresh_sq / size_sq) * direction
                size_sq = fresh_sq
        solved_ref[here, :] = solved
        parts = wide(solved)
        out_weights = mask_ref[b] * for_memory[:, here]
        if b:
            memory_high, memory_low = halves(memories_ref[0, b - 1])
            right = jnp.concatenate([twice(memory_high, 1), twice(memory_low, 1), pair], axis=0)
            found = dot_nt(parts, right)
            carried = (found[:, :STRETCH] + found[:, STRETCH:2 * STRETCH]) * keep
            scores = found[:, 2 * STRETCH:]
        else:
            carried = None
            scores = dot_nt(parts, pair)
        local = dot_nn(wide(scores * out_weights), twice(value_ref[here, :], 0))
        partial_ref[here, :] = local if carried is None else local + carried


def read_kernel(ids, solved_ref, partial_ref, seg_col_ref, in_memory_ref, out_ref):
    keep = same(seg_col_ref[...], ids[0])
    memory_high, memory_low = halves(in_memory_ref[0])
    right = jnp.concatenate([twice(memory_high, 1), twice(memory_low, 1)], axis=0)
    found = dot_nt(wide(solved_ref[...]), right)
    carried = (found[:, :STRETCH] + found[:, STRETCH:]) * keep
    out_ref[...] = (partial_ref[...] + carried).astype(out_ref.dtype)


def shifted(block, distance):
    count = lax.axis_size(AXES[0]) * lax.axis_size(AXES[1])
    route = [(i - distance, i) for i in range(count) if i >= distance]
    return lax.ppermute(block, AXES, route)


def gathered(local, first, last, last_1, last_3):
    reach = local + same(last_1, last) * shifted(local, 1)
    return same(last_1, first) * shifted(reach, 1) + same(last_3, first) * shifted(reach, 3)


def body(queries, key_vectors, value_vectors, write_gate, ridge_term, segment_ids):
    tokens, width = queries.shape
    heads = ridge_term.shape[0]
    size = width // heads
    blocks = tokens // STRETCH
    segs = segment_ids.reshape(1, tokens)
    seg_col = segment_ids.reshape(tokens, 1)
    smem = pl.BlockSpec(memory_space=pltpu.SMEM)
    column = pl.BlockSpec((tokens, size), lambda h: (0, h))

    def whole(*shape):
        return pl.BlockSpec(shape, lambda h: (0,) * len(shape))

    state = pl.BlockSpec((1, size, size), lambda h: (h, 0, 0))
    inner = pl.BlockSpec((1, blocks - 1, size, size), lambda h: (h, 0, 0, 0))
    rows = whole(heads, tokens)
    params = pltpu.CompilerParams(dimension_semantics=("arbitrary",), vmem_limit_bytes=VMEM_LIMIT)
    f32 = jnp.float32
    state_shape = jax.ShapeDtypeStruct((heads, size, size), f32)
    inner_shape = jax.ShapeDtypeStruct((heads, blocks - 1, size, size), f32)
    rows_shape = jax.ShapeDtypeStruct((heads, tokens), f32)
    flat_shape = jax.ShapeDtypeStruct((tokens, width), f32)
    gram, memory, grams, memories, for_gram, for_memory = pl.pallas_call(
        state_kernel,
        grid=(heads,),
        in_specs=[smem, column, column, rows, whole(1, tokens)],
        out_specs=[state, state, inner, inner, rows, rows],
        out_shape=[state_shape, state_shape, inner_shape, inner_shape, rows_shape, rows_shape],
        compiler_params=params,
        name="states",
    )(segment_ids, key_vectors, value_vectors, write_gate, segs)

    first, last = segment_ids[0].astype(f32), segment_ids[tokens - 1].astype(f32)
    last_1, last_3 = shifted(last, 1), shifted(last, 3)
    in_gram = gathered(gram, first, last, last_1, last_3)
    in_memory = gathered(memory, first, last, last_1, last_3)
    solved, partial = pl.pallas_call(
        solve_kernel,
        grid=(heads,),
        in_specs=[smem, smem, column, column, column, whole(tokens, 1), whole(1, tokens), rows, rows, state, inner, inner],
        out_specs=[column, column],
        out_shape=[flat_shape, flat_shape],
        scratch_shapes=[pltpu.VMEM((blocks, STRETCH, STRETCH), f32)],
        compiler_params=params,
        cost_estimate=pl.CostEstimate(flops=2 * 10**10, bytes_accessed=2 * 10**7, transcendentals=0),
        name="solve",
    )(segment_ids, ridge_term, queries, key_vectors, value_vectors, seg_col, segs, for_gram, for_memory, in_gram, grams, memories)
    return pl.pallas_call(
        read_kernel,
        grid=(heads,),
        in_specs=[smem, column, column, whole(tokens, 1), state],
        out_specs=column,
        out_shape=jax.ShapeDtypeStruct((tokens, width), jnp.bfloat16),
        compiler_params=params,
        name="read",
    )(segment_ids, solved, partial, seg_col, in_memory)


def solution(mesh):
    return jax.shard_map(
        body,
        mesh=mesh,
        in_specs=(
            P(AXES, None),
            P(AXES, None),
            P(AXES, None),
            P(None, AXES),
            P(),
            P(AXES),
        ),
        out_specs=P(AXES, None),
        check_vma=False,
    )
```

```python
import functools

import jax
import jax.numpy as jnp
from jax import lax
from jax.experimental import pallas as pl
from jax.experimental.pallas import tpu as pltpu
from jax.sharding import PartitionSpec as P

STRETCH = 128
HALF = 64
ITERS = 4
AXES = ("outer", "inner")
VMEM_LIMIT = 56 * 1024 * 1024
STATE_HEADS = 4
SOLVE_HEADS = 4
READ_HEADS = 6
f32 = jnp.float32


def halves(x):
    high = x.astype(jnp.bfloat16)
    return high, (x - high.astype(f32)).astype(jnp.bfloat16)


def twice(x, axis):
    return jnp.concatenate([x, x], axis=axis)


def wide(x):
    return jnp.concatenate(halves(x), axis=1)


def dot_nt(a, b):
    return lax.dot_general(a, b, (((1,), (1,)), ((), ())), preferred_element_type=f32)


def dot_nn(a, b):
    return lax.dot_general(a, b, (((1,), (0,)), ((), ())), preferred_element_type=f32)


def same(a, b):
    return (a == b).astype(f32)


def lanes_rows(rows):
    shape = (rows, STRETCH)
    return lax.broadcasted_iota(jnp.int32, shape, 1), lax.broadcasted_iota(jnp.int32, shape, 0)


def chain(ids, left_of, right_of, tails, blocks, out_ref, j):
    total = None
    for b in range(blocks):
        here = dot_nn(left_of(b, tails[b]), right_of(b))
        if b:
            here = here + same(ids[(b + 1) * STRETCH - 1], ids[b * STRETCH - 1]) * total
        total = here
        if b < blocks - 1:
            out_ref[j, b] = total
    return total


def gram_kernel(heads, ids, key_ref, gate_ref, segs_ref, packed_ref, grams_ref, wg_ref, wm_ref):
    tokens = key_ref.shape[0]
    blocks = tokens // STRETCH
    spans = [slice(b * STRETCH, (b + 1) * STRETCH) for b in range(blocks)]
    tails = [same(segs_ref[:, spans[b]], ids[(b + 1) * STRETCH - 1]) for b in range(blocks)]
    lane, row = lanes_rows(HALF)
    for j in range(STATE_HEADS):
        head = pl.program_id(0) * STATE_HEADS + j
        keys = key_ref[:, j * STRETCH:(j + 1) * STRETCH]
        keys_t = keys.astype(f32).T
        scale = lax.rsqrt(jnp.sum(keys_t * keys_t, axis=0, keepdims=True) + 1e-06)
        for_memory = gate_ref[pl.ds(head, 1), :] * scale
        for_gram = for_memory * scale
        wg_ref[pl.ds(head, 1), :] = for_gram
        wm_ref[pl.ds(head, 1), :] = for_memory
        gram = chain(
            ids,
            lambda b, tail: wide(keys_t[:, spans[b]] * (for_gram[:, spans[b]] * tail)),
            lambda b: twice(keys[spans[b]], 0),
            tails, blocks, grams_ref, j,
        )
        top, bottom = gram[:HALF], gram[HALF:]
        packed_ref[pl.ds(pl.multiple_of(head * HALF, HALF), HALF), :] = jnp.where(
            lane > row, top, pltpu.roll(bottom, HALF, 1)
        )
        packed_ref[pl.ds(heads * HALF + head, 1), :] = jnp.sum(
            jnp.where(lane == row, top, 0.0), axis=0, keepdims=True
        )

    @pl.when(pl.program_id(0) == 0)
    def _():
        rest = packed_ref.shape[0] - heads * HALF - heads
        packed_ref[pl.ds(heads * HALF + heads, rest), :] = jnp.full(
            (rest, STRETCH), ids[tokens - 1].astype(f32)
        )


def memory_kernel(ids, key_ref, value_ref, segs_ref, wm_ref, memory_ref, memories_ref):
    tokens = key_ref.shape[0]
    blocks = tokens // STRETCH
    spans = [slice(b * STRETCH, (b + 1) * STRETCH) for b in range(blocks)]
    tails = [same(segs_ref[:, spans[b]], ids[(b + 1) * STRETCH - 1]) for b in range(blocks)]
    for j in range(STATE_HEADS):
        head = pl.program_id(0) * STATE_HEADS + j
        columns = slice(j * STRETCH, (j + 1) * STRETCH)
        values_t = value_ref[:, columns].astype(f32).T
        for_memory = wm_ref[pl.ds(head, 1), :]
        memory_ref[j] = chain(
            ids,
            lambda b, tail: wide(values_t[:, spans[b]] * (for_memory[:, spans[b]] * tail)),
            lambda b: twice(key_ref[spans[b], columns], 0),
            tails, blocks, memories_ref, j,
        )


def unpacked(packed, corner):
    lane, row = lanes_rows(HALF)
    top = jnp.where(lane > row, packed, jnp.where(lane == row, 0.5 * corner, 0.0))
    low = jnp.where(lane < row, packed, jnp.where(lane == row, 0.5 * packed, 0.0))
    part = jnp.concatenate([top, pltpu.roll(low, HALF, 1)], axis=0)
    return part + part.T


def solve_kernel(heads, ids, ridge, query_ref, key_ref, value_ref, seg_col_ref, segs_ref, wg_ref, wm_ref, begun_ref, begun_end_ref, next_ref, next_end_ref, pair_ref, pair_end_ref, grams_ref, memories_ref, solved_ref, partial_ref, mask_ref):
    tokens = key_ref.shape[0]
    blocks = tokens // STRETCH
    every = [(j, b) for j in range(SOLVE_HEADS) for b in range(blocks)]
    spans = [slice(b * STRETCH, (b + 1) * STRETCH) for b in range(blocks)]
    first_head = pl.program_id(0) * SOLVE_HEADS

    @pl.when(pl.program_id(0) == 0)
    def _():
        lane, row = lanes_rows(STRETCH)
        for b in range(blocks):
            equal = seg_col_ref[spans[b], :] == segs_ref[:, spans[b]]
            mask_ref[b] = jnp.where((lane <= row) & equal, 1.0, 0.0)

    previous = [ids[max(b * STRETCH - 1, 0)] for b in range(blocks)]
    keep = [same(seg_col_ref[spans[b], :], previous[b]) for b in range(blocks)]
    first = ids[0].astype(f32)
    tag = heads
    take_next = same(next_end_ref[tag:tag + 1, :], first)
    take_pair = same(pair_end_ref[tag:tag + 1, :], first)
    incoming = []
    for j in range(SOLVE_HEADS):
        here = slice(j * HALF, (j + 1) * HALF)
        packed = begun_ref[here] + take_next * next_ref[here] + take_pair * pair_ref[here]
        at = pl.ds(first_head + j, 1)
        corner = begun_end_ref[at, :] + take_next * next_end_ref[at, :] + take_pair * pair_end_ref[at, :]
        incoming.append(unpacked(packed, corner))
    columns = [slice(j * STRETCH, (j + 1) * STRETCH) for j in range(SOLVE_HEADS)]
    lam = [ridge[first_head + j] for j in range(SOLVE_HEADS)]
    for_gram = [wg_ref[pl.ds(first_head + j, 1), :] for j in range(SOLVE_HEADS)]
    for_memory = [wm_ref[pl.ds(first_head + j, 1), :] for j in range(SOLVE_HEADS)]
    twin, keys_t, right, weights = {}, {}, {}, {}
    direction, residual, solved, size_sq = {}, {}, {}, {}
    for j, b in every:
        c = j, b
        keys = key_ref[spans[b], columns[j]]
        twin[c] = twice(keys, 0)
        keys_t[c] = twice(keys.T, 0)
        gram = incoming[j]
        if b:
            gram = grams_ref[j, b - 1] + same(previous[b], ids[0]) * gram
        gram_high, gram_low = halves(gram)
        right[c] = jnp.concatenate([twice(gram_high, 0), twice(gram_low, 0), keys_t[c]], axis=1)
        weights[c] = mask_ref[b] * for_gram[j][:, spans[b]]
        query = query_ref[spans[b], columns[j]].astype(f32)
        query = query * lax.rsqrt(jnp.sum(query * query, axis=1, keepdims=True) + 1e-06)
        direction[c] = residual[c] = query
        size_sq[c] = jnp.sum(query * query, axis=1, keepdims=True)
    for sweep in range(ITERS):
        found = {c: dot_nn(wide(direction[c]), right[c]) for c in every}
        for c in every:
            carried = (found[c][:, :STRETCH] + found[c][:, STRETCH:2 * STRETCH]) * keep[c[1]] + lam[c[0]] * direction[c]
            scores = found[c][:, 2 * STRETCH:]
            weighed = scores * weights[c]
            if sweep < ITERS - 1:
                image = carried + dot_nn(wide(weighed), twin[c])
            across = jnp.sum(weighed * scores + carried * direction[c], axis=1, keepdims=True)
            step = size_sq[c] / across
            move = step * direction[c]
            solved[c] = solved[c] + move if sweep else move
            if sweep < ITERS - 1:
                residual[c] = residual[c] - step * image
                fresh_sq = jnp.sum(residual[c] * residual[c], axis=1, keepdims=True)
                direction[c] = residual[c] + (fresh_sq / size_sq[c]) * direction[c]
                size_sq[c] = fresh_sq
    for j, b in every:
        c = j, b
        solved_ref[spans[b], columns[j]] = solved[c]
        parts = wide(solved[c])
        carried = None
        if b:
            memory_high, memory_low = halves(memories_ref[j, b - 1])
            found = dot_nt(parts, jnp.concatenate([twice(memory_high, 1), twice(memory_low, 1)], axis=0))
            carried = (found[:, :STRETCH] + found[:, STRETCH:]) * keep[b]
        scores = dot_nn(parts, keys_t[c]) * (mask_ref[b] * for_memory[j][:, spans[b]])
        local = dot_nn(wide(scores), twice(value_ref[spans[b], columns[j]], 0))
        partial_ref[spans[b], columns[j]] = local if carried is None else local + carried


def read_kernel(heads, ids, solved_ref, partial_ref, seg_col_ref, begun_ref, next_ref, next_end_ref, pair_ref, pair_end_ref, out_ref):
    first = ids[0].astype(f32)
    keep = same(seg_col_ref[...], ids[0])
    take_next = same(next_end_ref[heads:heads + 1, :], first)
    take_pair = same(pair_end_ref[heads:heads + 1, :], first)
    for j in range(READ_HEADS):
        columns = slice(j * STRETCH, (j + 1) * STRETCH)
        memory = begun_ref[j] + take_next * next_ref[j] + take_pair * pair_ref[j]
        memory_high, memory_low = halves(memory)
        right = jnp.concatenate([twice(memory_high, 1), twice(memory_low, 1)], axis=0)
        found = dot_nt(wide(solved_ref[:, columns]), right)
        carried = (found[:, :STRETCH] + found[:, STRETCH:]) * keep
        out_ref[:, columns] = (partial_ref[:, columns] + carried).astype(out_ref.dtype)


def moved(block, source):
    count = lax.axis_size(AXES[0]) * lax.axis_size(AXES[1])
    route = [(source(i), i) for i in range(count) if source(i) is not None and 0 <= source(i) < count]
    return lax.ppermute(block, AXES, route)


def first_round(local):
    across = moved(local, lambda i: i ^ 1)
    above = moved(local, lambda i: i - 4)
    return across, above


def second_round(pair, above):
    return moved(pair, lambda i: i - 1 - 2 * (i % 2)), moved(above, lambda i: None if i % 2 else i + 1)


def body(queries, key_vectors, value_vectors, write_gate, ridge_term, segment_ids):
    tokens, width = queries.shape
    heads = ridge_term.shape[0]
    size = width // heads
    blocks = tokens // STRETCH
    segs = segment_ids.reshape(1, tokens)
    seg_col = segment_ids.reshape(tokens, 1)
    smem = pl.BlockSpec(memory_space=pltpu.SMEM)
    ends = 16
    tag = heads * HALF + heads
    length = heads * HALF + ends

    def whole(*shape):
        return pl.BlockSpec(shape, lambda h: (0,) * len(shape))

    def column(n):
        return pl.BlockSpec((tokens, n * size), lambda h: (0, h))

    def state(n):
        return pl.BlockSpec((n, size, size), lambda h: (h, 0, 0))

    def inner(n):
        return pl.BlockSpec((n, blocks - 1, size, size), lambda h: (h, 0, 0, 0))

    def packed(n):
        return pl.BlockSpec((n * HALF, size), lambda h: (h, 0))

    end = pl.BlockSpec((ends, size), lambda h: (heads * HALF // ends, 0))
    rows = whole(heads, tokens)
    params = pltpu.CompilerParams(dimension_semantics=("arbitrary",), vmem_limit_bytes=VMEM_LIMIT)

    def shaped(*shape):
        return jax.ShapeDtypeStruct(shape, f32)

    def cost(flops, moved_bytes):
        return pl.CostEstimate(flops=flops, bytes_accessed=moved_bytes, transcendentals=0)

    gram, grams, for_gram, for_memory = pl.pallas_call(
        functools.partial(gram_kernel, heads),
        grid=(heads // STATE_HEADS,),
        in_specs=[smem, column(STATE_HEADS), rows, whole(1, tokens)],
        out_specs=[whole(length, size), inner(STATE_HEADS), rows, rows],
        out_shape=[shaped(length, size), shaped(heads, blocks - 1, size, size), shaped(heads, tokens), shaped(heads, tokens)],
        compiler_params=params,
        name="grams",
    )(segment_ids, key_vectors, write_gate, segs)
    across, above = first_round(gram)
    memory, memories = pl.pallas_call(
        memory_kernel,
        grid=(heads // STATE_HEADS,),
        in_specs=[smem, column(STATE_HEADS), column(STATE_HEADS), whole(1, tokens), rows],
        out_specs=[state(STATE_HEADS), inner(STATE_HEADS)],
        out_shape=[shaped(heads, size, size), shaped(heads, blocks - 1, size, size)],
        compiler_params=params,
        cost_estimate=cost(10**9, 10**7),
        name="memories",
    )(segment_ids, key_vectors, value_vectors, segs, for_memory)
    across_m, above_m = first_round(memory)

    odd = lax.axis_index(AXES) % 2 == 1
    first = segment_ids[0].astype(f32)
    equal = same(gram[tag:tag + 1], across[tag:tag + 1])
    take_across = same(across[tag:tag + 1], first) * odd.astype(f32)
    take_above = same(above[tag:tag + 1], first)
    is_tag = lax.broadcasted_iota(jnp.int32, gram.shape, 0) >= tag
    later, earlier = jnp.where(odd, gram, across), jnp.where(odd, across, gram)
    pair = later + jnp.where(is_tag, 0.0, equal) * earlier
    begun = take_above * above + take_across * across
    pair, nxt = second_round(pair, above)
    later, earlier = jnp.where(odd, memory, across_m), jnp.where(odd, across_m, memory)
    pair_m = later + equal * earlier
    begun_m = take_above * above_m + take_across * across_m
    pair_m, nxt_m = second_round(pair_m, above_m)

    solved, partial = pl.pallas_call(
        functools.partial(solve_kernel, heads),
        grid=(heads // SOLVE_HEADS,),
        in_specs=[smem, smem, column(SOLVE_HEADS), column(SOLVE_HEADS), column(SOLVE_HEADS), whole(tokens, 1), whole(1, tokens), rows, rows]
        + [packed(SOLVE_HEADS), end] * 3
        + [inner(SOLVE_HEADS), inner(SOLVE_HEADS)],
        out_specs=[column(SOLVE_HEADS), column(SOLVE_HEADS)],
        out_shape=[shaped(tokens, width), shaped(tokens, width)],
        scratch_shapes=[pltpu.VMEM((blocks, STRETCH, STRETCH), f32)],
        compiler_params=params,
        cost_estimate=cost(2 * 10**10, 2 * 10**7),
        name="solve",
    )(segment_ids, ridge_term, queries, key_vectors, value_vectors, seg_col, segs, for_gram, for_memory, begun, begun, nxt, nxt, pair, pair, grams, memories)
    return pl.pallas_call(
        functools.partial(read_kernel, heads),
        grid=(heads // READ_HEADS,),
        in_specs=[smem, column(READ_HEADS), column(READ_HEADS), whole(tokens, 1), state(READ_HEADS), state(READ_HEADS), end, state(READ_HEADS), end],
        out_specs=column(READ_HEADS),
        out_shape=jax.ShapeDtypeStruct((tokens, width), jnp.bfloat16),
        compiler_params=params,
        name="read",
    )(segment_ids, solved, partial, seg_col, begun_m, nxt_m, nxt, pair_m, pair)


def solution(mesh):
    return jax.shard_map(
        body,
        mesh=mesh,
        in_specs=(
            P(AXES, None),
            P(AXES, None),
            P(AXES, None),
            P(None, AXES),
            P(),
            P(AXES),
        ),
        out_specs=P(AXES, None),
        check_vma=False,
    )
```

```python
import functools

import jax
import jax.numpy as jnp
from jax import lax
from jax.experimental import pallas as pl
from jax.experimental.pallas import tpu as pltpu
from jax.sharding import PartitionSpec as P

STRETCH = 128
HALF = 64
ITERS = 4
AXES = ("outer", "inner")
VMEM_LIMIT = 28 * 1024 * 1024
STATE_HEADS = 4
SOLVE_HEADS = 4
READ_HEADS = 6
f32 = jnp.float32


def halves(x):
    high = x.astype(jnp.bfloat16)
    return high, (x - high.astype(f32)).astype(jnp.bfloat16)


def twice(x, axis):
    return jnp.concatenate([x, x], axis=axis)


def wide(x):
    return jnp.concatenate(halves(x), axis=1)


def dot_nt(a, b):
    return lax.dot_general(a, b, (((1,), (1,)), ((), ())), preferred_element_type=f32)


def dot_nn(a, b):
    return lax.dot_general(a, b, (((1,), (0,)), ((), ())), preferred_element_type=f32)


def row_of(ref):
    return ref[...].reshape(1, ref.shape[0])


def down(row):
    return jnp.broadcast_to(row.astype(f32), (row.shape[1], row.shape[1])).T


def same(a, b):
    return (a == b).astype(f32)


def lanes_rows(rows):
    shape = (rows, STRETCH)
    return lax.broadcasted_iota(jnp.int32, shape, 1), lax.broadcasted_iota(jnp.int32, shape, 0)


def chain(ids, left_of, right_of, tails, blocks, out_ref, j):
    total = None
    for b in range(blocks):
        here = dot_nn(left_of(b, tails[b]), right_of(b))
        if b:
            here = here + same(ids[(b + 1) * STRETCH - 1], ids[b * STRETCH - 1]) * total
        total = here
        if b < blocks - 1:
            out_ref[j, b] = total
    return total


def gram_kernel(heads, ids, key_ref, gate_ref, segs_ref, packed_ref, grams_ref, wg_ref, wm_ref):
    tokens = key_ref.shape[0]
    blocks = tokens // STRETCH
    segs = row_of(segs_ref)
    spans = [slice(b * STRETCH, (b + 1) * STRETCH) for b in range(blocks)]
    tails = [same(segs[:, spans[b]], ids[(b + 1) * STRETCH - 1]) for b in range(blocks)]
    lane, row = lanes_rows(HALF)
    for j in range(STATE_HEADS):
        head = pl.program_id(0) * STATE_HEADS + j
        keys = key_ref[:, j * STRETCH:(j + 1) * STRETCH]
        keys_t = keys.astype(f32).T
        scale = lax.rsqrt(jnp.sum(keys_t * keys_t, axis=0, keepdims=True) + 1e-06)
        for_memory = gate_ref[pl.ds(head, 1), :] * scale
        for_gram = for_memory * scale
        wg_ref[pl.ds(head, 1), :] = for_gram
        wm_ref[pl.ds(head, 1), :] = for_memory
        gram = chain(
            ids,
            lambda b, tail: wide(keys_t[:, spans[b]] * (for_gram[:, spans[b]] * tail)),
            lambda b: twice(keys[spans[b]], 0),
            tails, blocks, grams_ref, j,
        )
        top, bottom = gram[:HALF], gram[HALF:]
        packed_ref[pl.ds(pl.multiple_of(head * HALF, HALF), HALF), :] = jnp.where(
            lane > row, top, pltpu.roll(bottom, HALF, 1)
        )
        packed_ref[pl.ds(heads * HALF + head, 1), :] = jnp.sum(
            jnp.where(lane == row, top, 0.0), axis=0, keepdims=True
        )

    @pl.when(pl.program_id(0) == 0)
    def _():
        rest = packed_ref.shape[0] - heads * HALF - heads
        packed_ref[pl.ds(heads * HALF + heads, rest), :] = jnp.full(
            (rest, STRETCH), ids[tokens - 1].astype(f32)
        )


def memory_kernel(ids, key_ref, value_ref, segs_ref, wm_ref, memory_ref, memories_ref):
    tokens = key_ref.shape[0]
    blocks = tokens // STRETCH
    segs = row_of(segs_ref)
    spans = [slice(b * STRETCH, (b + 1) * STRETCH) for b in range(blocks)]
    tails = [same(segs[:, spans[b]], ids[(b + 1) * STRETCH - 1]) for b in range(blocks)]
    for j in range(STATE_HEADS):
        head = pl.program_id(0) * STATE_HEADS + j
        columns = slice(j * STRETCH, (j + 1) * STRETCH)
        values_t = value_ref[:, columns].astype(f32).T
        for_memory = wm_ref[pl.ds(head, 1), :]
        memory_ref[j] = chain(
            ids,
            lambda b, tail: wide(values_t[:, spans[b]] * (for_memory[:, spans[b]] * tail)),
            lambda b: twice(key_ref[spans[b], columns], 0),
            tails, blocks, memories_ref, j,
        )


def unpacked(packed, corner):
    lane, row = lanes_rows(HALF)
    top = jnp.where(lane > row, packed, jnp.where(lane == row, 0.5 * corner, 0.0))
    low = jnp.where(lane < row, packed, jnp.where(lane == row, 0.5 * packed, 0.0))
    part = jnp.concatenate([top, pltpu.roll(low, HALF, 1)], axis=0)
    return part + part.T


def pair_kernel(tag, odd, local_ref, across_ref, pair_ref):
    is_odd = jnp.full((1, STRETCH), odd[0], jnp.int32) == 1
    local, across = local_ref[...], across_ref[...]
    equal = same(local_ref[tag:tag + 1, :], across_ref[tag:tag + 1, :])
    later = jnp.where(is_odd, local, across)
    earlier = jnp.where(is_odd, across, local)
    pair_ref[...] = later + equal * earlier
    pair_ref[tag:, :] = jnp.where(is_odd, local_ref[tag:, :], across_ref[tag:, :])


def normed(query):
    query = query.astype(f32)
    return query * lax.rsqrt(jnp.sum(query * query, axis=1, keepdims=True) + 1e-06)


def tables(ids, segs_ref, mask_ref, keep_ref):
    blocks = mask_ref.shape[0]

    @pl.when(pl.program_id(0) == 0)
    def _():
        segs = row_of(segs_ref)
        lane, row = lanes_rows(STRETCH)
        for b in range(blocks):
            here = segs[:, b * STRETCH:(b + 1) * STRETCH]
            below = down(here)
            mask_ref[b] = jnp.where((lane <= row) & (below == here.astype(f32)), 1.0, 0.0)
            keep_ref[b] = same(below, ids[max(b * STRETCH - 1, 0)].astype(f32))


def open_kernel(ids, ridge, query_ref, key_ref, segs_ref, wg_ref, grams_ref, image_ref, mask_ref, keep_ref):
    blocks = key_ref.shape[0] // STRETCH
    tables(ids, segs_ref, mask_ref, keep_ref)
    for j in range(SOLVE_HEADS):
        head = pl.program_id(0) * SOLVE_HEADS + j
        columns = slice(j * STRETCH, (j + 1) * STRETCH)
        for_gram = wg_ref[pl.ds(head, 1), :]
        for b in range(blocks):
            span = slice(b * STRETCH, (b + 1) * STRETCH)
            keys = key_ref[span, columns]
            query = normed(query_ref[span, columns])
            parts = wide(query)
            right = twice(keys.T, 0)
            image = ridge[head] * query
            if b:
                gram_high, gram_low = halves(grams_ref[j, b - 1])
                right = jnp.concatenate([right, twice(gram_high, 0), twice(gram_low, 0)], axis=1)
            found = dot_nn(parts, right)
            if b:
                image = image + (found[:, STRETCH:2 * STRETCH] + found[:, 2 * STRETCH:]) * keep_ref[b]
            weighed = found[:, :STRETCH] * (mask_ref[b] * for_gram[:, span])
            image_ref[span, columns] = image + dot_nn(wide(weighed), twice(keys, 0))


def solve_kernel(heads, ids, ridge, odd, query_ref, key_ref, value_ref, segs_ref, wg_ref, wm_ref, image_ref, across_ref, across_end_ref, above_ref, above_end_ref, next_ref, next_end_ref, pair_ref, pair_end_ref, grams_ref, memories_ref, solved_ref, partial_ref, mask_ref, keep_ref):
    blocks = key_ref.shape[0] // STRETCH
    every = [(j, b) for j in range(SOLVE_HEADS) for b in range(blocks)]
    spans = [slice(b * STRETCH, (b + 1) * STRETCH) for b in range(blocks)]
    columns = [slice(j * STRETCH, (j + 1) * STRETCH) for j in range(SOLVE_HEADS)]
    first_head = pl.program_id(0) * SOLVE_HEADS
    tables(ids, segs_ref, mask_ref, keep_ref)
    first = ids[0].astype(f32)
    arrived = [(across_ref, across_end_ref, odd[0].astype(f32)), (above_ref, above_end_ref, 1.0), (next_ref, next_end_ref, 1.0), (pair_ref, pair_end_ref, 1.0)]
    takes = [same(end[heads:heads + 1, :], first) * use for _, end, use in arrived]
    incoming = []
    for j in range(SOLVE_HEADS):
        here = slice(j * HALF, (j + 1) * HALF)
        at = pl.ds(first_head + j, 1)
        packed = corner = 0.0
        for take, (ref, end, _) in zip(takes, arrived):
            packed = packed + take * ref[here]
            corner = corner + take * end[at, :]
        incoming.append(unpacked(packed, corner))
    lam = [ridge[first_head + j] for j in range(SOLVE_HEADS)]
    for_gram = [wg_ref[pl.ds(first_head + j, 1), :] for j in range(SOLVE_HEADS)]
    for_memory = [wm_ref[pl.ds(first_head + j, 1), :] for j in range(SOLVE_HEADS)]
    joins = [same(ids[max(b * STRETCH - 1, 0)], ids[0]) for b in range(blocks)]
    twin, keys_t, right, weights = {}, {}, {}, {}
    direction, residual, solved, size_sq = {}, {}, {}, {}
    enter = []
    for j in range(SOLVE_HEADS):
        gram_high, gram_low = halves(incoming[j])
        enter.append(jnp.concatenate([twice(gram_high, 0), twice(gram_low, 0)], axis=1))
    query = {c: normed(query_ref[spans[c[1]], columns[c[0]]]) for c in every}
    found = {c: dot_nn(wide(query[c]), enter[c[0]]) for c in every}
    for c in every:
        j, b = c
        keys = key_ref[spans[b], columns[j]]
        twin[c] = twice(keys, 0)
        keys_t[c] = twice(keys.T, 0)
        weights[c] = mask_ref[b] * for_gram[j][:, spans[b]]
        if b:
            high, low = halves(grams_ref[j, b - 1] + joins[b] * incoming[j])
            right[c] = jnp.concatenate([twice(high, 0), twice(low, 0), keys_t[c]], axis=1)
        else:
            right[c] = jnp.concatenate([enter[j], keys_t[c]], axis=1)
    for c in every:
        j, b = c
        image = image_ref[spans[b], columns[j]] + (found[c][:, :STRETCH] + found[c][:, STRETCH:]) * (keep_ref[b] * joins[b])
        first_sq = jnp.sum(query[c] * query[c], axis=1, keepdims=True)
        step = first_sq / jnp.sum(query[c] * image, axis=1, keepdims=True)
        solved[c] = step * query[c]
        residual[c] = query[c] - step * image
        size_sq[c] = jnp.sum(residual[c] * residual[c], axis=1, keepdims=True)
        direction[c] = residual[c] + (size_sq[c] / first_sq) * query[c]
    for sweep in range(1, ITERS):
        found = {c: dot_nn(wide(direction[c]), right[c]) for c in every}
        for c in every:
            carried = (found[c][:, :STRETCH] + found[c][:, STRETCH:2 * STRETCH]) * keep_ref[c[1]] + lam[c[0]] * direction[c]
            scores = found[c][:, 2 * STRETCH:]
            weighed = scores * weights[c]
            if sweep < ITERS - 1:
                image = carried + dot_nn(wide(weighed), twin[c])
            step = size_sq[c] / jnp.sum(weighed * scores + carried * direction[c], axis=1, keepdims=True)
            solved[c] = solved[c] + step * direction[c]
            if sweep < ITERS - 1:
                residual[c] = residual[c] - step * image
                fresh_sq = jnp.sum(residual[c] * residual[c], axis=1, keepdims=True)
                direction[c] = residual[c] + (fresh_sq / size_sq[c]) * direction[c]
                size_sq[c] = fresh_sq
    parts = {c: wide(solved[c]) for c in every}
    scores = {c: dot_nn(parts[c], keys_t[c]) for c in every}
    found = {}
    for j, b in every:
        if b:
            high, low = halves(memories_ref[j, b - 1])
            found[j, b] = dot_nt(parts[j, b], jnp.concatenate([twice(high, 1), twice(low, 1)], axis=0))
    for j, b in every:
        c = j, b
        solved_ref[spans[b], columns[j]] = solved[c]
        weighed = scores[c] * (mask_ref[b] * for_memory[j][:, spans[b]])
        local = dot_nn(wide(weighed), twice(value_ref[spans[b], columns[j]], 0))
        if b:
            local = local + (found[c][:, :STRETCH] + found[c][:, STRETCH:]) * keep_ref[b]
        partial_ref[spans[b], columns[j]] = local


def read_kernel(heads, ids, solved_ref, partial_ref, segs_ref, begun_ref, next_ref, next_end_ref, pair_ref, pair_end_ref, out_ref):
    first = ids[0].astype(f32)
    segs = row_of(segs_ref)
    blocks = segs.shape[1] // STRETCH
    keep = jnp.concatenate([same(down(segs[:, b * STRETCH:(b + 1) * STRETCH]), first) for b in range(blocks)], axis=0)
    take_next = same(next_end_ref[heads:heads + 1, :], first)
    take_pair = same(pair_end_ref[heads:heads + 1, :], first)
    for j in range(READ_HEADS):
        columns = slice(j * STRETCH, (j + 1) * STRETCH)
        memory = begun_ref[j] + take_next * next_ref[j] + take_pair * pair_ref[j]
        memory_high, memory_low = halves(memory)
        right = jnp.concatenate([twice(memory_high, 1), twice(memory_low, 1)], axis=0)
        found = dot_nt(wide(solved_ref[:, columns]), right)
        carried = (found[:, :STRETCH] + found[:, STRETCH:]) * keep
        out_ref[:, columns] = (partial_ref[:, columns] + carried).astype(out_ref.dtype)


def moved(block, source):
    count = lax.axis_size(AXES[0]) * lax.axis_size(AXES[1])
    route = [(source(i), i) for i in range(count) if source(i) is not None and 0 <= source(i) < count]
    return lax.ppermute(block, AXES, route)


def first_round(local):
    across = moved(local, lambda i: i ^ 1)
    above = moved(local, lambda i: i - 4)
    return across, above


def second_round(pair, above):
    return moved(pair, lambda i: i - 1 - 2 * (i % 2)), moved(above, lambda i: None if i % 2 else i + 1)


def body(queries, key_vectors, value_vectors, write_gate, ridge_term, segment_ids):
    tokens, width = queries.shape
    heads = ridge_term.shape[0]
    size = width // heads
    blocks = tokens // STRETCH
    smem = pl.BlockSpec(memory_space=pltpu.SMEM)
    ends = 16
    tag = heads * HALF + heads
    length = heads * HALF + ends

    def whole(*shape):
        return pl.BlockSpec(shape, lambda h: (0,) * len(shape))

    def column(n):
        return pl.BlockSpec((tokens, n * size), lambda h: (0, h))

    def state(n):
        return pl.BlockSpec((n, size, size), lambda h: (h, 0, 0))

    def inner(n):
        return pl.BlockSpec((n, blocks - 1, size, size), lambda h: (h, 0, 0, 0))

    def packed(n):
        return pl.BlockSpec((n * HALF, size), lambda h: (h, 0))

    end = pl.BlockSpec((ends, size), lambda h: (heads * HALF // ends, 0))
    rows = whole(heads, tokens)
    params = pltpu.CompilerParams(dimension_semantics=("arbitrary",), vmem_limit_bytes=VMEM_LIMIT)

    def shaped(*shape):
        return jax.ShapeDtypeStruct(shape, f32)

    def cost(flops, moved_bytes):
        return pl.CostEstimate(flops=flops, bytes_accessed=moved_bytes, transcendentals=0)

    gram, grams, for_gram, for_memory = pl.pallas_call(
        functools.partial(gram_kernel, heads),
        grid=(heads // STATE_HEADS,),
        in_specs=[smem, column(STATE_HEADS), rows, whole(tokens)],
        out_specs=[whole(length, size), inner(STATE_HEADS), rows, rows],
        out_shape=[shaped(length, size), shaped(heads, blocks - 1, size, size), shaped(heads, tokens), shaped(heads, tokens)],
        compiler_params=params,
        name="grams",
    )(segment_ids, key_vectors, write_gate, segment_ids)
    across, above = first_round(gram)
    memory, memories = pl.pallas_call(
        memory_kernel,
        grid=(heads // STATE_HEADS,),
        in_specs=[smem, column(STATE_HEADS), column(STATE_HEADS), whole(tokens), rows],
        out_specs=[state(STATE_HEADS), inner(STATE_HEADS)],
        out_shape=[shaped(heads, size, size), shaped(heads, blocks - 1, size, size)],
        compiler_params=params,
        cost_estimate=cost(10**9, 10**7),
        name="memories",
    )(segment_ids, key_vectors, value_vectors, segment_ids, for_memory)
    across_m, above_m = first_round(memory)

    odd = (lax.axis_index(AXES) % 2).astype(jnp.int32).reshape(1)
    vmem = pl.BlockSpec(memory_space=pltpu.VMEM)
    pair = pl.pallas_call(
        functools.partial(pair_kernel, tag),
        in_specs=[smem, vmem, vmem],
        out_specs=vmem,
        out_shape=shaped(length, size),
        name="pair",
    )(odd, gram, across)
    pair, above, queries = lax.optimization_barrier((pair, above, queries))
    pair_in, next_in = second_round(pair, above)

    tables = [pltpu.VMEM((blocks, STRETCH, STRETCH), f32), pltpu.VMEM((blocks, STRETCH, STRETCH), f32)]
    image = pl.pallas_call(
        open_kernel,
        grid=(heads // SOLVE_HEADS,),
        in_specs=[smem, smem, column(SOLVE_HEADS), column(SOLVE_HEADS), whole(tokens), rows, inner(SOLVE_HEADS)],
        out_specs=column(SOLVE_HEADS),
        out_shape=shaped(tokens, width),
        scratch_shapes=tables,
        compiler_params=params,
        cost_estimate=cost(4 * 10**9, 10**7),
        name="open",
    )(segment_ids, ridge_term, queries, key_vectors, segment_ids, for_gram, grams)

    is_odd = odd[0] == 1
    first = segment_ids[0].astype(f32)
    equal = same(gram[tag:tag + 1], across[tag:tag + 1])
    pair_m = jnp.where(is_odd, memory, across_m) + equal * jnp.where(is_odd, across_m, memory)
    pair_m, above_m, across_m, image = lax.optimization_barrier((pair_m, above_m, across_m, image))
    pair_m_in, next_m_in = second_round(pair_m, above_m)
    take_across = same(across[tag:tag + 1], first) * is_odd.astype(f32)
    take_above = same(above[tag:tag + 1], first)
    begun_m = take_above * above_m + take_across * across_m

    solved, partial = pl.pallas_call(
        functools.partial(solve_kernel, heads),
        grid=(heads // SOLVE_HEADS,),
        in_specs=[smem, smem, smem, column(SOLVE_HEADS), column(SOLVE_HEADS), column(SOLVE_HEADS), whole(tokens), rows, rows, column(SOLVE_HEADS)]
        + [packed(SOLVE_HEADS), end] * 4
        + [inner(SOLVE_HEADS), inner(SOLVE_HEADS)],
        out_specs=[column(SOLVE_HEADS), column(SOLVE_HEADS)],
        out_shape=[shaped(tokens, width), shaped(tokens, width)],
        scratch_shapes=tables,
        compiler_params=params,
        cost_estimate=cost(2 * 10**10, 2 * 10**7),
        name="solve",
    )(
        segment_ids, ridge_term, odd, queries, key_vectors, value_vectors, segment_ids, for_gram, for_memory, image,
        across, across, above, above, next_in, next_in, pair_in, pair_in, grams, memories,
    )
    return pl.pallas_call(
        functools.partial(read_kernel, heads),
        grid=(heads // READ_HEADS,),
        in_specs=[smem, column(READ_HEADS), column(READ_HEADS), whole(tokens), state(READ_HEADS), state(READ_HEADS), end, state(READ_HEADS), end],
        out_specs=column(READ_HEADS),
        out_shape=jax.ShapeDtypeStruct((tokens, width), jnp.bfloat16),
        compiler_params=params,
        name="read",
    )(segment_ids, solved, partial, segment_ids, begun_m, next_m_in, next_in, pair_m_in, pair_in)


def solution(mesh):
    return jax.shard_map(
        body,
        mesh=mesh,
        in_specs=(
            P(AXES, None),
            P(AXES, None),
            P(AXES, None),
            P(None, AXES),
            P(),
            P(AXES),
        ),
        out_specs=P(AXES, None),
        check_vma=False,
    )
```

```python
import functools

import jax
import jax.numpy as jnp
from jax import lax
from jax.experimental import pallas as pl
from jax.experimental.pallas import tpu as pltpu
from jax.sharding import PartitionSpec as P

STRETCH = 128
HALF = 64
ITERS = 4
AXES = ("outer", "inner")
MIB = 1024 * 1024
STATE_HEADS = 6
SOLVE_HEADS = 3
READ_HEADS = 6
f32 = jnp.float32


def halves(x):
    high = x.astype(jnp.bfloat16)
    return high, (x - high.astype(f32)).astype(jnp.bfloat16)


def twice(x, axis):
    return jnp.concatenate([x, x], axis=axis)


def wide(x):
    return jnp.concatenate(halves(x), axis=1)


def dot_nt(a, b):
    return lax.dot_general(a, b, (((1,), (1,)), ((), ())), preferred_element_type=f32)


def dot_nn(a, b):
    return lax.dot_general(a, b, (((1,), (0,)), ((), ())), preferred_element_type=f32)


def row_of(ref):
    return ref[...].reshape(1, ref.shape[0])


def down(row):
    return jnp.broadcast_to(row.astype(f32), (row.shape[1], row.shape[1])).T


def same(a, b):
    return (a == b).astype(f32)


def lanes_rows(rows):
    shape = (rows, STRETCH)
    return lax.broadcasted_iota(jnp.int32, shape, 1), lax.broadcasted_iota(jnp.int32, shape, 0)


def chain(ids, left_of, right_of, tails, blocks, out_ref, j):
    total = None
    for b in range(blocks):
        here = dot_nn(left_of(b, tails[b]), right_of(b))
        if b:
            here = here + same(ids[(b + 1) * STRETCH - 1], ids[b * STRETCH - 1]) * total
        total = here
        if b < blocks - 1:
            out_ref[j, b] = total
    return total


def gram_kernel(heads, ids, key_ref, gate_ref, segs_ref, packed_ref, grams_ref, wg_ref, wm_ref):
    tokens = key_ref.shape[0]
    blocks = tokens // STRETCH
    segs = row_of(segs_ref)
    spans = [slice(b * STRETCH, (b + 1) * STRETCH) for b in range(blocks)]
    tails = [same(segs[:, spans[b]], ids[(b + 1) * STRETCH - 1]) for b in range(blocks)]
    lane, row = lanes_rows(HALF)
    for j in range(STATE_HEADS):
        head = pl.program_id(0) * STATE_HEADS + j
        keys = key_ref[:, j * STRETCH:(j + 1) * STRETCH]
        keys_t = keys.astype(f32).T
        scale = lax.rsqrt(jnp.sum(keys_t * keys_t, axis=0, keepdims=True) + 1e-06)
        for_memory = gate_ref[pl.ds(head, 1), :] * scale
        for_gram = for_memory * scale
        wg_ref[pl.ds(head, 1), :] = for_gram
        wm_ref[pl.ds(head, 1), :] = for_memory
        gram = chain(
            ids,
            lambda b, tail: wide(keys_t[:, spans[b]] * (for_gram[:, spans[b]] * tail)),
            lambda b: twice(keys[spans[b]], 0),
            tails, blocks, grams_ref, j,
        )
        top, bottom = gram[:HALF], gram[HALF:]
        packed_ref[pl.ds(pl.multiple_of(head * HALF, HALF), HALF), :] = jnp.where(
            lane > row, top, pltpu.roll(bottom, HALF, 1)
        )
        packed_ref[pl.ds(heads * HALF + head, 1), :] = jnp.sum(
            jnp.where(lane == row, top, 0.0), axis=0, keepdims=True
        )

    @pl.when(pl.program_id(0) == 0)
    def _():
        rest = packed_ref.shape[0] - heads * HALF - heads
        packed_ref[pl.ds(heads * HALF + heads, rest), :] = jnp.full(
            (rest, STRETCH), ids[tokens - 1].astype(f32)
        )


def memory_kernel(ids, key_ref, value_ref, segs_ref, wm_ref, memory_ref, memories_ref):
    tokens = key_ref.shape[0]
    blocks = tokens // STRETCH
    segs = row_of(segs_ref)
    spans = [slice(b * STRETCH, (b + 1) * STRETCH) for b in range(blocks)]
    tails = [same(segs[:, spans[b]], ids[(b + 1) * STRETCH - 1]) for b in range(blocks)]
    for j in range(STATE_HEADS):
        head = pl.program_id(0) * STATE_HEADS + j
        columns = slice(j * STRETCH, (j + 1) * STRETCH)
        values_t = value_ref[:, columns].astype(f32).T
        for_memory = wm_ref[pl.ds(head, 1), :]
        memory_ref[j] = chain(
            ids,
            lambda b, tail: wide(values_t[:, spans[b]] * (for_memory[:, spans[b]] * tail)),
            lambda b: twice(key_ref[spans[b], columns], 0),
            tails, blocks, memories_ref, j,
        )


def unpacked(packed, corner):
    lane, row = lanes_rows(HALF)
    top = jnp.where(lane > row, packed, jnp.where(lane == row, 0.5 * corner, 0.0))
    low = jnp.where(lane < row, packed, jnp.where(lane == row, 0.5 * packed, 0.0))
    part = jnp.concatenate([top, pltpu.roll(low, HALF, 1)], axis=0)
    return part + part.T


def pair_kernel(tag, odd, local_ref, across_ref, pair_ref):
    is_odd = jnp.full((1, STRETCH), odd[0], jnp.int32) == 1
    local, across = local_ref[...], across_ref[...]
    equal = same(local_ref[tag:tag + 1, :], across_ref[tag:tag + 1, :])
    later = jnp.where(is_odd, local, across)
    earlier = jnp.where(is_odd, across, local)
    pair_ref[...] = later + equal * earlier
    pair_ref[tag:, :] = jnp.where(is_odd, local_ref[tag:, :], across_ref[tag:, :])


def pair_memory_kernel(heads, tag, odd, tag_ref, across_tag_ref, local_ref, across_ref, pair_ref):
    is_odd = jnp.full((1, STRETCH), odd[0], jnp.int32) == 1
    equal = same(tag_ref[tag:tag + 1, :], across_tag_ref[tag:tag + 1, :])
    of_local, of_across = jnp.where(is_odd, 1.0, equal), jnp.where(is_odd, equal, 1.0)
    for j in range(heads):
        pair_ref[j] = of_local * local_ref[j] + of_across * across_ref[j]


def normed(query):
    query = query.astype(f32)
    return query * lax.rsqrt(jnp.sum(query * query, axis=1, keepdims=True) + 1e-06)


def tables(ids, segs_ref, mask_ref, keep_ref):
    blocks = mask_ref.shape[0]

    @pl.when(pl.program_id(0) == 0)
    def _():
        segs = row_of(segs_ref)
        lane, row = lanes_rows(STRETCH)
        for b in range(blocks):
            here = segs[:, b * STRETCH:(b + 1) * STRETCH]
            below = down(here)
            mask_ref[b] = jnp.where((lane <= row) & (below == here.astype(f32)), 1.0, 0.0)
            keep_ref[b] = same(below, ids[max(b * STRETCH - 1, 0)].astype(f32))


def open_kernel(ids, ridge, query_ref, key_ref, segs_ref, wg_ref, grams_ref, image_ref, mask_ref, keep_ref):
    blocks = key_ref.shape[0] // STRETCH
    tables(ids, segs_ref, mask_ref, keep_ref)
    for j in range(SOLVE_HEADS):
        head = pl.program_id(0) * SOLVE_HEADS + j
        columns = slice(j * STRETCH, (j + 1) * STRETCH)
        for_gram = wg_ref[pl.ds(head, 1), :]
        for b in range(blocks):
            span = slice(b * STRETCH, (b + 1) * STRETCH)
            keys = key_ref[span, columns]
            query = normed(query_ref[span, columns])
            parts = wide(query)
            right = twice(keys.T, 0)
            image = ridge[head] * query
            if b:
                gram_high, gram_low = halves(grams_ref[j, b - 1])
                right = jnp.concatenate([right, twice(gram_high, 0), twice(gram_low, 0)], axis=1)
            found = dot_nn(parts, right)
            if b:
                image = image + (found[:, STRETCH:2 * STRETCH] + found[:, 2 * STRETCH:]) * keep_ref[b]
            weighed = found[:, :STRETCH] * (mask_ref[b] * for_gram[:, span])
            image_ref[span, columns] = image + dot_nn(wide(weighed), twice(keys, 0))


def solve_kernel(heads, ids, ridge, odd, query_ref, key_ref, value_ref, segs_ref, wg_ref, wm_ref, image_ref, across_ref, across_end_ref, above_ref, above_end_ref, next_ref, next_end_ref, pair_ref, pair_end_ref, grams_ref, memories_ref, solved_ref, partial_ref, mask_ref, keep_ref):
    blocks = key_ref.shape[0] // STRETCH
    every = [(j, b) for j in range(SOLVE_HEADS) for b in range(blocks)]
    spans = [slice(b * STRETCH, (b + 1) * STRETCH) for b in range(blocks)]
    columns = [slice(j * STRETCH, (j + 1) * STRETCH) for j in range(SOLVE_HEADS)]
    first_head = pl.program_id(0) * SOLVE_HEADS
    tables(ids, segs_ref, mask_ref, keep_ref)
    first = ids[0].astype(f32)
    arrived = [(across_ref, across_end_ref, odd[0].astype(f32)), (above_ref, above_end_ref, 1.0), (next_ref, next_end_ref, 1.0), (pair_ref, pair_end_ref, 1.0)]
    takes = [same(end[heads:heads + 1, :], first) * use for _, end, use in arrived]
    incoming = []
    for j in range(SOLVE_HEADS):
        here = slice(j * HALF, (j + 1) * HALF)
        at = pl.ds(first_head + j, 1)
        packed = corner = 0.0
        for take, (ref, end, _) in zip(takes, arrived):
            packed = packed + take * ref[here]
            corner = corner + take * end[at, :]
        incoming.append(unpacked(packed, corner))
    lam = [ridge[first_head + j] for j in range(SOLVE_HEADS)]
    for_gram = [wg_ref[pl.ds(first_head + j, 1), :] for j in range(SOLVE_HEADS)]
    for_memory = [wm_ref[pl.ds(first_head + j, 1), :] for j in range(SOLVE_HEADS)]
    joins = [same(ids[max(b * STRETCH - 1, 0)], ids[0]) for b in range(blocks)]
    twin, keys_t, right, weights = {}, {}, {}, {}
    direction, residual, solved, size_sq = {}, {}, {}, {}
    enter = []
    for j in range(SOLVE_HEADS):
        gram_high, gram_low = halves(incoming[j])
        enter.append(jnp.concatenate([twice(gram_high, 0), twice(gram_low, 0)], axis=1))
    query = {c: normed(query_ref[spans[c[1]], columns[c[0]]]) for c in every}
    found = {c: dot_nn(wide(query[c]), enter[c[0]]) for c in every}
    for c in every:
        j, b = c
        keys = key_ref[spans[b], columns[j]]
        twin[c] = twice(keys, 0)
        keys_t[c] = twice(keys.T, 0)
        weights[c] = mask_ref[b] * for_gram[j][:, spans[b]]
        if b:
            high, low = halves(grams_ref[j, b - 1] + joins[b] * incoming[j])
            right[c] = jnp.concatenate([twice(high, 0), twice(low, 0), keys_t[c]], axis=1)
        else:
            right[c] = jnp.concatenate([enter[j], keys_t[c]], axis=1)
    for c in every:
        j, b = c
        image = image_ref[spans[b], columns[j]] + (found[c][:, :STRETCH] + found[c][:, STRETCH:]) * (keep_ref[b] * joins[b])
        first_sq = jnp.sum(query[c] * query[c], axis=1, keepdims=True)
        step = first_sq / jnp.sum(query[c] * image, axis=1, keepdims=True)
        solved[c] = step * query[c]
        residual[c] = query[c] - step * image
        size_sq[c] = jnp.sum(residual[c] * residual[c], axis=1, keepdims=True)
        direction[c] = residual[c] + (size_sq[c] / first_sq) * query[c]
    for sweep in range(1, ITERS):
        found = {c: dot_nn(wide(direction[c]), right[c]) for c in every}
        for c in every:
            carried = (found[c][:, :STRETCH] + found[c][:, STRETCH:2 * STRETCH]) * keep_ref[c[1]] + lam[c[0]] * direction[c]
            scores = found[c][:, 2 * STRETCH:]
            weighed = scores * weights[c]
            if sweep < ITERS - 1:
                image = carried + dot_nn(wide(weighed), twin[c])
            step = size_sq[c] / jnp.sum(weighed * scores + carried * direction[c], axis=1, keepdims=True)
            solved[c] = solved[c] + step * direction[c]
            if sweep < ITERS - 1:
                residual[c] = residual[c] - step * image
                fresh_sq = jnp.sum(residual[c] * residual[c], axis=1, keepdims=True)
                direction[c] = residual[c] + (fresh_sq / size_sq[c]) * direction[c]
                size_sq[c] = fresh_sq
    parts = {c: wide(solved[c]) for c in every}
    scores = {c: dot_nn(parts[c], keys_t[c]) for c in every}
    found = {}
    for j, b in every:
        if b:
            high, low = halves(memories_ref[j, b - 1])
            found[j, b] = dot_nt(parts[j, b], jnp.concatenate([twice(high, 1), twice(low, 1)], axis=0))
    for j, b in every:
        c = j, b
        solved_ref[spans[b], columns[j]] = solved[c]
        weighed = scores[c] * (mask_ref[b] * for_memory[j][:, spans[b]])
        local = dot_nn(wide(weighed), twice(value_ref[spans[b], columns[j]], 0))
        if b:
            local = local + (found[c][:, :STRETCH] + found[c][:, STRETCH:]) * keep_ref[b]
        partial_ref[spans[b], columns[j]] = local


def read_kernel(heads, ids, odd, solved_ref, partial_ref, segs_ref, across_ref, across_end_ref, above_ref, above_end_ref, next_ref, next_end_ref, pair_ref, pair_end_ref, out_ref):
    first = ids[0].astype(f32)
    segs = row_of(segs_ref)
    blocks = segs.shape[1] // STRETCH
    keep = jnp.concatenate([same(down(segs[:, b * STRETCH:(b + 1) * STRETCH]), first) for b in range(blocks)], axis=0)
    arrived = [(across_ref, across_end_ref, odd[0].astype(f32)), (above_ref, above_end_ref, 1.0), (next_ref, next_end_ref, 1.0), (pair_ref, pair_end_ref, 1.0)]
    takes = [same(end[heads:heads + 1, :], first) * use for _, end, use in arrived]
    for j in range(READ_HEADS):
        columns = slice(j * STRETCH, (j + 1) * STRETCH)
        memory = 0.0
        for take, (ref, _, _) in zip(takes, arrived):
            memory = memory + take * ref[j]
        memory_high, memory_low = halves(memory)
        right = jnp.concatenate([twice(memory_high, 1), twice(memory_low, 1)], axis=0)
        found = dot_nt(wide(solved_ref[:, columns]), right)
        carried = (found[:, :STRETCH] + found[:, STRETCH:]) * keep
        out_ref[:, columns] = (partial_ref[:, columns] + carried).astype(out_ref.dtype)


def moved(block, source):
    count = lax.axis_size(AXES[0]) * lax.axis_size(AXES[1])
    route = [(source(i), i) for i in range(count) if source(i) is not None and 0 <= source(i) < count]
    return lax.ppermute(block, AXES, route)


def first_round(local):
    across = moved(local, lambda i: i ^ 1)
    above = moved(local, lambda i: i - 4)
    return across, above


def paired(pair):
    return moved(pair, lambda i: i - 1 - 2 * (i % 2))


def handed(above):
    return moved(above, lambda i: None if i % 2 else i + 1)


def body(queries, key_vectors, value_vectors, write_gate, ridge_term, segment_ids):
    tokens, width = queries.shape
    heads = ridge_term.shape[0]
    size = width // heads
    blocks = tokens // STRETCH
    smem = pl.BlockSpec(memory_space=pltpu.SMEM)
    ends = 16
    tag = heads * HALF + heads
    length = heads * HALF + ends

    def whole(*shape):
        return pl.BlockSpec(shape, lambda h: (0,) * len(shape))

    def column(n):
        return pl.BlockSpec((tokens, n * size), lambda h: (0, h))

    def state(n):
        return pl.BlockSpec((n, size, size), lambda h: (h, 0, 0))

    def inner(n):
        return pl.BlockSpec((n, blocks - 1, size, size), lambda h: (h, 0, 0, 0))

    def packed(n):
        return pl.BlockSpec((n * HALF, size), lambda h: (h, 0))

    end = pl.BlockSpec((ends, size), lambda h: (heads * HALF // ends, 0))
    rows = whole(heads, tokens)

    def grant(mebibytes):
        return pltpu.CompilerParams(vmem_limit_bytes=mebibytes * MIB)

    def shaped(*shape):
        return jax.ShapeDtypeStruct(shape, f32)

    def cost(flops, moved_bytes):
        return pl.CostEstimate(flops=flops, bytes_accessed=moved_bytes, transcendentals=0)

    gram, grams, for_gram, for_memory = pl.pallas_call(
        functools.partial(gram_kernel, heads),
        grid=(heads // STATE_HEADS,),
        in_specs=[smem, column(STATE_HEADS), rows, whole(tokens)],
        out_specs=[whole(length, size), inner(STATE_HEADS), rows, rows],
        out_shape=[shaped(length, size), shaped(heads, blocks - 1, size, size), shaped(heads, tokens), shaped(heads, tokens)],
        compiler_params=grant(56),
        name="grams",
    )(segment_ids, key_vectors, write_gate, segment_ids)
    across, above = first_round(gram)
    memory, memories = pl.pallas_call(
        memory_kernel,
        grid=(heads // STATE_HEADS,),
        in_specs=[smem, column(STATE_HEADS), column(STATE_HEADS), whole(tokens), rows],
        out_specs=[state(STATE_HEADS), inner(STATE_HEADS)],
        out_shape=[shaped(heads, size, size), shaped(heads, blocks - 1, size, size)],
        compiler_params=grant(56),
        cost_estimate=cost(10**9, 10**7),
        name="memories",
    )(segment_ids, key_vectors, value_vectors, segment_ids, for_memory)
    across_m, above_m = first_round(memory)

    odd = (lax.axis_index(AXES) % 2).astype(jnp.int32).reshape(1)
    vmem = pl.BlockSpec(memory_space=pltpu.VMEM)
    pair = pl.pallas_call(
        functools.partial(pair_kernel, tag),
        in_specs=[smem, vmem, vmem],
        out_specs=vmem,
        out_shape=shaped(length, size),
        compiler_params=grant(8),
        name="pair",
    )(odd, gram, across)
    pair, above, queries = lax.optimization_barrier((pair, above, queries))
    pair_in, next_in = paired(pair), handed(above)

    tables = [pltpu.VMEM((blocks, STRETCH, STRETCH), f32), pltpu.VMEM((blocks, STRETCH, STRETCH), f32)]
    image = pl.pallas_call(
        open_kernel,
        grid=(heads // SOLVE_HEADS,),
        in_specs=[smem, smem, column(SOLVE_HEADS), column(SOLVE_HEADS), whole(tokens), rows, inner(SOLVE_HEADS)],
        out_specs=column(SOLVE_HEADS),
        out_shape=shaped(tokens, width),
        scratch_shapes=tables,
        compiler_params=grant(28),
        cost_estimate=cost(4 * 10**9, 10**7),
        name="open",
    )(segment_ids, ridge_term, queries, key_vectors, segment_ids, for_gram, grams)

    pair_m = pl.pallas_call(
        functools.partial(pair_memory_kernel, heads, tag),
        in_specs=[smem, vmem, vmem, vmem, vmem],
        out_specs=vmem,
        out_shape=shaped(heads, size, size),
        compiler_params=grant(8),
        name="pair_memory",
    )(odd, gram, across, memory, across_m)
    above_m, image = lax.optimization_barrier((above_m, image))
    next_m_in = handed(above_m)
    pair_m, pair_in = lax.optimization_barrier((pair_m, pair_in))
    pair_m_in = paired(pair_m)

    solved, partial = pl.pallas_call(
        functools.partial(solve_kernel, heads),
        grid=(heads // SOLVE_HEADS,),
        in_specs=[smem, smem, smem, column(SOLVE_HEADS), column(SOLVE_HEADS), column(SOLVE_HEADS), whole(tokens), rows, rows, column(SOLVE_HEADS)]
        + [packed(SOLVE_HEADS), end] * 4
        + [inner(SOLVE_HEADS), inner(SOLVE_HEADS)],
        out_specs=[column(SOLVE_HEADS), column(SOLVE_HEADS)],
        out_shape=[shaped(tokens, width), shaped(tokens, width)],
        scratch_shapes=tables,
        compiler_params=grant(20),
        cost_estimate=cost(2 * 10**10, 2 * 10**7),
        name="solve",
    )(
        segment_ids, ridge_term, odd, queries, key_vectors, value_vectors, segment_ids, for_gram, for_memory, image,
        across, across, above, above, next_in, next_in, pair_in, pair_in, grams, memories,
    )
    return pl.pallas_call(
        functools.partial(read_kernel, heads),
        grid=(heads // READ_HEADS,),
        in_specs=[smem, smem, column(READ_HEADS), column(READ_HEADS), whole(tokens)] + [state(READ_HEADS), end] * 4,
        out_specs=column(READ_HEADS),
        out_shape=jax.ShapeDtypeStruct((tokens, width), jnp.bfloat16),
        compiler_params=grant(16),
        name="read",
    )(segment_ids, odd, solved, partial, segment_ids, across_m, across, above_m, above, next_m_in, next_in, pair_m_in, pair_in)


def solution(mesh):
    return jax.shard_map(
        body,
        mesh=mesh,
        in_specs=(
            P(AXES, None),
            P(AXES, None),
            P(AXES, None),
            P(None, AXES),
            P(),
            P(AXES),
        ),
        out_specs=P(AXES, None),
        check_vma=False,
    )
```

```python
import functools

import jax
import jax.numpy as jnp
from jax import lax
from jax.experimental import pallas as pl
from jax.experimental.pallas import tpu as pltpu
from jax.sharding import PartitionSpec as P

STRETCH = 128
HALF = 64
ITERS = 4
AXES = ("outer", "inner")
MIB = 1024 * 1024
STATE_HEADS = 6
SOLVE_HEADS = 3
READ_HEADS = 6
f32 = jnp.float32


def halves(x):
    high = x.astype(jnp.bfloat16)
    return high, (x - high.astype(f32)).astype(jnp.bfloat16)


def twice(x, axis):
    return jnp.concatenate([x, x], axis=axis)


def wide(x):
    return jnp.concatenate(halves(x), axis=1)


def dot_nt(a, b):
    return lax.dot_general(a, b, (((1,), (1,)), ((), ())), preferred_element_type=f32)


def dot_nn(a, b):
    return lax.dot_general(a, b, (((1,), (0,)), ((), ())), preferred_element_type=f32)


def row_of(ref):
    return ref[...].reshape(1, ref.shape[0])


def down(row):
    return jnp.broadcast_to(row.astype(f32), (row.shape[1], row.shape[1])).T


def same(a, b):
    return (a == b).astype(f32)


def lanes_rows(rows):
    shape = (rows, STRETCH)
    return lax.broadcasted_iota(jnp.int32, shape, 1), lax.broadcasted_iota(jnp.int32, shape, 0)


def chain(ids, left_of, right_of, tails, blocks, out_ref, j):
    total = None
    for b in range(blocks):
        here = dot_nn(left_of(b, tails[b]), right_of(b))
        if b:
            here = here + same(ids[(b + 1) * STRETCH - 1], ids[b * STRETCH - 1]) * total
        total = here
        if b < blocks - 1:
            out_ref[j, b] = total
    return total


def gram_kernel(heads, ids, key_ref, gate_ref, segs_ref, packed_ref, grams_ref, wg_ref, wm_ref):
    tokens = key_ref.shape[0]
    blocks = tokens // STRETCH
    segs = row_of(segs_ref)
    spans = [slice(b * STRETCH, (b + 1) * STRETCH) for b in range(blocks)]
    tails = [same(segs[:, spans[b]], ids[(b + 1) * STRETCH - 1]) for b in range(blocks)]
    lane, row = lanes_rows(HALF)
    for j in range(STATE_HEADS):
        head = pl.program_id(0) * STATE_HEADS + j
        keys = key_ref[:, j * STRETCH:(j + 1) * STRETCH]
        keys_t = keys.astype(f32).T
        scale = lax.rsqrt(jnp.sum(keys_t * keys_t, axis=0, keepdims=True) + 1e-06)
        for_memory = gate_ref[pl.ds(head, 1), :] * scale
        for_gram = for_memory * scale
        wg_ref[pl.ds(head, 1), :] = for_gram
        wm_ref[pl.ds(head, 1), :] = for_memory
        gram = chain(
            ids,
            lambda b, tail: wide(keys_t[:, spans[b]] * (for_gram[:, spans[b]] * tail)),
            lambda b: twice(keys[spans[b]], 0),
            tails, blocks, grams_ref, j,
        )
        top, bottom = gram[:HALF], gram[HALF:]
        packed_ref[pl.ds(pl.multiple_of(head * HALF, HALF), HALF), :] = jnp.where(
            lane > row, top, pltpu.roll(bottom, HALF, 1)
        )
        packed_ref[pl.ds(heads * HALF + head, 1), :] = jnp.sum(
            jnp.where(lane == row, top, 0.0), axis=0, keepdims=True
        )

    @pl.when(pl.program_id(0) == 0)
    def _():
        rest = packed_ref.shape[0] - heads * HALF - heads
        packed_ref[pl.ds(heads * HALF + heads, rest), :] = jnp.full(
            (rest, STRETCH), ids[tokens - 1].astype(f32)
        )


def memory_kernel(ids, key_ref, value_ref, segs_ref, wm_ref, memory_ref, memories_ref):
    tokens = key_ref.shape[0]
    blocks = tokens // STRETCH
    segs = row_of(segs_ref)
    spans = [slice(b * STRETCH, (b + 1) * STRETCH) for b in range(blocks)]
    tails = [same(segs[:, spans[b]], ids[(b + 1) * STRETCH - 1]) for b in range(blocks)]
    for j in range(STATE_HEADS):
        head = pl.program_id(0) * STATE_HEADS + j
        columns = slice(j * STRETCH, (j + 1) * STRETCH)
        values_t = value_ref[:, columns].astype(f32).T
        for_memory = wm_ref[pl.ds(head, 1), :]
        memory_ref[j] = chain(
            ids,
            lambda b, tail: wide(values_t[:, spans[b]] * (for_memory[:, spans[b]] * tail)),
            lambda b: twice(key_ref[spans[b], columns], 0),
            tails, blocks, memories_ref, j,
        )


def unpacked(packed, corner):
    lane, row = lanes_rows(HALF)
    top = jnp.where(lane > row, packed, jnp.where(lane == row, 0.5 * corner, 0.0))
    low = jnp.where(lane < row, packed, jnp.where(lane == row, 0.5 * packed, 0.0))
    part = jnp.concatenate([top, pltpu.roll(low, HALF, 1)], axis=0)
    return part + part.T


def pair_kernel(tag, odd, local_ref, across_ref, pair_ref):
    is_odd = jnp.full((1, STRETCH), odd[0], jnp.int32) == 1
    local, across = local_ref[...], across_ref[...]
    equal = same(local_ref[tag:tag + 1, :], across_ref[tag:tag + 1, :])
    later = jnp.where(is_odd, local, across)
    earlier = jnp.where(is_odd, across, local)
    pair_ref[...] = later + equal * earlier
    pair_ref[tag:, :] = jnp.where(is_odd, local_ref[tag:, :], across_ref[tag:, :])


def pair_memory_kernel(heads, tag, odd, tag_ref, across_tag_ref, local_ref, across_ref, pair_ref):
    is_odd = jnp.full((1, STRETCH), odd[0], jnp.int32) == 1
    equal = same(tag_ref[tag:tag + 1, :], across_tag_ref[tag:tag + 1, :])
    of_local, of_across = jnp.where(is_odd, 1.0, equal), jnp.where(is_odd, equal, 1.0)
    for j in range(heads):
        pair_ref[j] = of_local * local_ref[j] + of_across * across_ref[j]


def normed(query):
    query = query.astype(f32)
    return query * lax.rsqrt(jnp.sum(query * query, axis=1, keepdims=True) + 1e-06)


def tables(ids, segs_ref, mask_ref, keep_ref):
    blocks = mask_ref.shape[0]

    @pl.when(pl.program_id(0) == 0)
    def _():
        segs = row_of(segs_ref)
        lane, row = lanes_rows(STRETCH)
        for b in range(blocks):
            here = segs[:, b * STRETCH:(b + 1) * STRETCH]
            below = down(here)
            mask_ref[b] = jnp.where((lane <= row) & (below == here.astype(f32)), 1.0, 0.0)
            keep_ref[b] = same(below, ids[max(b * STRETCH - 1, 0)].astype(f32))


def open_kernel(ids, ridge, query_ref, key_ref, segs_ref, wg_ref, grams_ref, image_ref, mask_ref, keep_ref):
    blocks = key_ref.shape[0] // STRETCH
    tables(ids, segs_ref, mask_ref, keep_ref)
    for j in range(SOLVE_HEADS):
        head = pl.program_id(0) * SOLVE_HEADS + j
        columns = slice(j * STRETCH, (j + 1) * STRETCH)
        for_gram = wg_ref[pl.ds(head, 1), :]
        for b in range(blocks):
            span = slice(b * STRETCH, (b + 1) * STRETCH)
            keys = key_ref[span, columns]
            query = normed(query_ref[span, columns])
            parts = wide(query)
            right = twice(keys.T, 0)
            image = ridge[head] * query
            if b:
                gram_high, gram_low = halves(grams_ref[j, b - 1])
                right = jnp.concatenate([right, twice(gram_high, 0), twice(gram_low, 0)], axis=1)
            found = dot_nn(parts, right)
            if b:
                image = image + (found[:, STRETCH:2 * STRETCH] + found[:, 2 * STRETCH:]) * keep_ref[b]
            weighed = found[:, :STRETCH] * (mask_ref[b] * for_gram[:, span])
            image_ref[span, columns] = image + dot_nn(wide(weighed), twice(keys, 0))


def solve_kernel(heads, ids, ridge, odd, query_ref, key_ref, value_ref, segs_ref, wg_ref, wm_ref, image_ref, across_ref, across_end_ref, above_ref, above_end_ref, next_ref, next_end_ref, pair_ref, pair_end_ref, grams_ref, memories_ref, solved_ref, partial_ref, mask_ref, keep_ref):
    blocks = key_ref.shape[0] // STRETCH
    every = [(j, b) for j in range(SOLVE_HEADS) for b in range(blocks)]
    spans = [slice(b * STRETCH, (b + 1) * STRETCH) for b in range(blocks)]
    columns = [slice(j * STRETCH, (j + 1) * STRETCH) for j in range(SOLVE_HEADS)]
    first_head = pl.program_id(0) * SOLVE_HEADS
    tables(ids, segs_ref, mask_ref, keep_ref)
    first = ids[0].astype(f32)
    arrived = [(across_ref, across_end_ref, odd[0].astype(f32)), (above_ref, above_end_ref, 1.0), (next_ref, next_end_ref, 1.0), (pair_ref, pair_end_ref, 1.0)]
    takes = [same(end[heads:heads + 1, :], first) * use for _, end, use in arrived]
    incoming = []
    for j in range(SOLVE_HEADS):
        here = slice(j * HALF, (j + 1) * HALF)
        at = pl.ds(first_head + j, 1)
        packed = corner = 0.0
        for take, (ref, end, _) in zip(takes, arrived):
            packed = packed + take * ref[here]
            corner = corner + take * end[at, :]
        incoming.append(unpacked(packed, corner))
    lam = [ridge[first_head + j] for j in range(SOLVE_HEADS)]
    for_gram = [wg_ref[pl.ds(first_head + j, 1), :] for j in range(SOLVE_HEADS)]
    for_memory = [wm_ref[pl.ds(first_head + j, 1), :] for j in range(SOLVE_HEADS)]
    joins = [same(ids[max(b * STRETCH - 1, 0)], ids[0]) for b in range(blocks)]
    twin, keys_t, right, weights = {}, {}, {}, {}
    direction, residual, solved, size_sq = {}, {}, {}, {}
    enter = []
    for j in range(SOLVE_HEADS):
        gram_high, gram_low = halves(incoming[j])
        enter.append(jnp.concatenate([twice(gram_high, 0), twice(gram_low, 0)], axis=1))
    query = {c: normed(query_ref[spans[c[1]], columns[c[0]]]) for c in every}
    found = {c: dot_nn(wide(query[c]), enter[c[0]]) for c in every}
    for c in every:
        j, b = c
        keys = key_ref[spans[b], columns[j]]
        twin[c] = twice(keys, 0)
        keys_t[c] = twice(keys.T, 0)
        weights[c] = mask_ref[b] * for_gram[j][:, spans[b]]
        if b:
            high, low = halves(grams_ref[j, b - 1] + joins[b] * incoming[j])
            right[c] = jnp.concatenate([twice(high, 0), twice(low, 0), keys_t[c]], axis=1)
        else:
            right[c] = jnp.concatenate([enter[j], keys_t[c]], axis=1)
    for c in every:
        j, b = c
        image = image_ref[spans[b], columns[j]] + (found[c][:, :STRETCH] + found[c][:, STRETCH:]) * (keep_ref[b] * joins[b])
        first_sq = jnp.sum(query[c] * query[c], axis=1, keepdims=True)
        step = first_sq / jnp.sum(query[c] * image, axis=1, keepdims=True)
        solved[c] = step * query[c]
        residual[c] = query[c] - step * image
        size_sq[c] = jnp.sum(residual[c] * residual[c], axis=1, keepdims=True)
        direction[c] = residual[c] + (size_sq[c] / first_sq) * query[c]
    for sweep in range(1, ITERS):
        found = {c: dot_nn(wide(direction[c]), right[c]) for c in every}
        for c in every:
            carried = (found[c][:, :STRETCH] + found[c][:, STRETCH:2 * STRETCH]) * keep_ref[c[1]] + lam[c[0]] * direction[c]
            scores = found[c][:, 2 * STRETCH:]
            weighed = scores * weights[c]
            if sweep < ITERS - 1:
                image = carried + dot_nn(wide(weighed), twin[c])
            step = size_sq[c] / jnp.sum(weighed * scores + carried * direction[c], axis=1, keepdims=True)
            solved[c] = solved[c] + step * direction[c]
            if sweep < ITERS - 1:
                residual[c] = residual[c] - step * image
                fresh_sq = jnp.sum(residual[c] * residual[c], axis=1, keepdims=True)
                direction[c] = residual[c] + (fresh_sq / size_sq[c]) * direction[c]
                size_sq[c] = fresh_sq
    parts = {c: wide(solved[c]) for c in every}
    scores = {c: dot_nn(parts[c], keys_t[c]) for c in every}
    found = {}
    for j, b in every:
        if b:
            high, low = halves(memories_ref[j, b - 1])
            found[j, b] = dot_nt(parts[j, b], jnp.concatenate([twice(high, 1), twice(low, 1)], axis=0))
    for j, b in every:
        c = j, b
        solved_ref[spans[b], columns[j]] = solved[c]
        weighed = scores[c] * (mask_ref[b] * for_memory[j][:, spans[b]])
        local = dot_nn(wide(weighed), twice(value_ref[spans[b], columns[j]], 0))
        if b:
            local = local + (found[c][:, :STRETCH] + found[c][:, STRETCH:]) * keep_ref[b]
        partial_ref[spans[b], columns[j]] = local


def read_kernel(heads, ids, odd, solved_ref, partial_ref, segs_ref, across_ref, across_end_ref, above_ref, above_end_ref, next_ref, next_end_ref, pair_ref, pair_end_ref, far_ref, out_ref):
    first = ids[0].astype(f32)
    segs = row_of(segs_ref)
    blocks = segs.shape[1] // STRETCH
    keep = jnp.concatenate([same(down(segs[:, b * STRETCH:(b + 1) * STRETCH]), first) for b in range(blocks)], axis=0)
    arrived = [(across_ref, across_end_ref, odd[0].astype(f32)), (above_ref, above_end_ref, 1.0), (next_ref, next_end_ref, 1.0), (pair_ref, pair_end_ref, 1.0), (far_ref, pair_end_ref, 1.0)]
    takes = [same(end[heads:heads + 1, :], first) * use for _, end, use in arrived]
    for j in range(READ_HEADS):
        columns = slice(j * STRETCH, (j + 1) * STRETCH)
        memory = 0.0
        for take, (ref, _, _) in zip(takes, arrived):
            memory = memory + take * ref[j]
        memory_high, memory_low = halves(memory)
        right = jnp.concatenate([twice(memory_high, 1), twice(memory_low, 1)], axis=0)
        found = dot_nt(wide(solved_ref[:, columns]), right)
        carried = (found[:, :STRETCH] + found[:, STRETCH:]) * keep
        out_ref[:, columns] = (partial_ref[:, columns] + carried).astype(out_ref.dtype)


def moved(block, source):
    count = lax.axis_size(AXES[0]) * lax.axis_size(AXES[1])
    route = [(source(i), i) for i in range(count) if source(i) is not None and 0 <= source(i) < count]
    return lax.ppermute(block, AXES, route)


def first_round(local):
    across = moved(local, lambda i: i ^ 1)
    above = moved(local, lambda i: i - 4)
    return across, above


def crosses(i):
    return i % 16 < 2


def paired(pair, wanted=lambda i: True):
    return moved(pair, lambda i: i - 1 - 2 * (i % 2) if wanted(i) else None)


def handed(above):
    return moved(above, lambda i: None if i % 2 else i + 1)


def body(queries, key_vectors, value_vectors, write_gate, ridge_term, segment_ids):
    tokens, width = queries.shape
    heads = ridge_term.shape[0]
    size = width // heads
    blocks = tokens // STRETCH
    smem = pl.BlockSpec(memory_space=pltpu.SMEM)
    ends = 16
    tag = heads * HALF + heads
    length = heads * HALF + ends

    def whole(*shape):
        return pl.BlockSpec(shape, lambda h: (0,) * len(shape))

    def column(n):
        return pl.BlockSpec((tokens, n * size), lambda h: (0, h))

    def state(n):
        return pl.BlockSpec((n, size, size), lambda h: (h, 0, 0))

    def inner(n):
        return pl.BlockSpec((n, blocks - 1, size, size), lambda h: (h, 0, 0, 0))

    def packed(n):
        return pl.BlockSpec((n * HALF, size), lambda h: (h, 0))

    end = pl.BlockSpec((ends, size), lambda h: (heads * HALF // ends, 0))
    rows = whole(heads, tokens)

    def grant(mebibytes):
        return pltpu.CompilerParams(vmem_limit_bytes=mebibytes * MIB)

    def shaped(*shape):
        return jax.ShapeDtypeStruct(shape, f32)

    def cost(flops, moved_bytes):
        return pl.CostEstimate(flops=flops, bytes_accessed=moved_bytes, transcendentals=0)

    gram, grams, for_gram, for_memory = pl.pallas_call(
        functools.partial(gram_kernel, heads),
        grid=(heads // STATE_HEADS,),
        in_specs=[smem, column(STATE_HEADS), rows, whole(tokens)],
        out_specs=[whole(length, size), inner(STATE_HEADS), rows, rows],
        out_shape=[shaped(length, size), shaped(heads, blocks - 1, size, size), shaped(heads, tokens), shaped(heads, tokens)],
        compiler_params=grant(56),
        name="grams",
    )(segment_ids, key_vectors, write_gate, segment_ids)
    across, above = first_round(gram)
    memory, memories = pl.pallas_call(
        memory_kernel,
        grid=(heads // STATE_HEADS,),
        in_specs=[smem, column(STATE_HEADS), column(STATE_HEADS), whole(tokens), rows],
        out_specs=[state(STATE_HEADS), inner(STATE_HEADS)],
        out_shape=[shaped(heads, size, size), shaped(heads, blocks - 1, size, size)],
        compiler_params=grant(56),
        cost_estimate=cost(10**9, 10**7),
        name="memories",
    )(segment_ids, key_vectors, value_vectors, segment_ids, for_memory)
    across_m, above_m = first_round(memory)

    odd = (lax.axis_index(AXES) % 2).astype(jnp.int32).reshape(1)
    vmem = pl.BlockSpec(memory_space=pltpu.VMEM)
    pair = pl.pallas_call(
        functools.partial(pair_kernel, tag),
        in_specs=[smem, vmem, vmem],
        out_specs=vmem,
        out_shape=shaped(length, size),
        compiler_params=grant(8),
        name="pair",
    )(odd, gram, across)
    pair, above, queries = lax.optimization_barrier((pair, above, queries))
    pair_in, next_in = paired(pair), handed(above)

    tables = [pltpu.VMEM((blocks, STRETCH, STRETCH), f32), pltpu.VMEM((blocks, STRETCH, STRETCH), f32)]
    image = pl.pallas_call(
        open_kernel,
        grid=(heads // SOLVE_HEADS,),
        in_specs=[smem, smem, column(SOLVE_HEADS), column(SOLVE_HEADS), whole(tokens), rows, inner(SOLVE_HEADS)],
        out_specs=column(SOLVE_HEADS),
        out_shape=shaped(tokens, width),
        scratch_shapes=tables,
        compiler_params=grant(28),
        cost_estimate=cost(4 * 10**9, 10**7),
        name="open",
    )(segment_ids, ridge_term, queries, key_vectors, segment_ids, for_gram, grams)

    pair_m = pl.pallas_call(
        functools.partial(pair_memory_kernel, heads, tag),
        in_specs=[smem, vmem, vmem, vmem, vmem],
        out_specs=vmem,
        out_shape=shaped(heads, size, size),
        compiler_params=grant(8),
        name="pair_memory",
    )(odd, gram, across, memory, across_m)
    pair_m, above_m, image = lax.optimization_barrier((pair_m, above_m, image))
    next_m_in = handed(above_m)
    near_m_in = paired(pair_m, lambda i: not crosses(i))
    pair_m, pair_in = lax.optimization_barrier((pair_m, pair_in))
    far_m_in = paired(pair_m, crosses)

    solved, partial = pl.pallas_call(
        functools.partial(solve_kernel, heads),
        grid=(heads // SOLVE_HEADS,),
        in_specs=[smem, smem, smem, column(SOLVE_HEADS), column(SOLVE_HEADS), column(SOLVE_HEADS), whole(tokens), rows, rows, column(SOLVE_HEADS)]
        + [packed(SOLVE_HEADS), end] * 4
        + [inner(SOLVE_HEADS), inner(SOLVE_HEADS)],
        out_specs=[column(SOLVE_HEADS), column(SOLVE_HEADS)],
        out_shape=[shaped(tokens, width), shaped(tokens, width)],
        scratch_shapes=tables,
        compiler_params=grant(20),
        cost_estimate=cost(2 * 10**10, 2 * 10**7),
        name="solve",
    )(
        segment_ids, ridge_term, odd, queries, key_vectors, value_vectors, segment_ids, for_gram, for_memory, image,
        across, across, above, above, next_in, next_in, pair_in, pair_in, grams, memories,
    )
    return pl.pallas_call(
        functools.partial(read_kernel, heads),
        grid=(heads // READ_HEADS,),
        in_specs=[smem, smem, column(READ_HEADS), column(READ_HEADS), whole(tokens)] + [state(READ_HEADS), end] * 4 + [state(READ_HEADS)],
        out_specs=column(READ_HEADS),
        out_shape=jax.ShapeDtypeStruct((tokens, width), jnp.bfloat16),
        compiler_params=grant(16),
        name="read",
    )(segment_ids, odd, solved, partial, segment_ids, across_m, across, above_m, above, next_m_in, next_in, near_m_in, pair_in, far_m_in)


def solution(mesh):
    return jax.shard_map(
        body,
        mesh=mesh,
        in_specs=(
            P(AXES, None),
            P(AXES, None),
            P(AXES, None),
            P(None, AXES),
            P(),
            P(AXES),
        ),
        out_specs=P(AXES, None),
        check_vma=False,
    )
```

```python
import functools

import jax
import jax.numpy as jnp
from jax import lax
from jax.experimental import pallas as pl
from jax.experimental.pallas import tpu as pltpu
from jax.sharding import PartitionSpec as P

STRETCH = 128
HALF = 64
ITERS = 4
AXES = ("outer", "inner")
MIB = 1024 * 1024
STATE_HEADS = 6
SOLVE_HEADS = 3
READ_HEADS = 6
f32 = jnp.float32


def halves(x):
    high = x.astype(jnp.bfloat16)
    return high, (x - high.astype(f32)).astype(jnp.bfloat16)


def twice(x, axis):
    return jnp.concatenate([x, x], axis=axis)


def wide(x):
    return jnp.concatenate(halves(x), axis=1)


def dot_nt(a, b):
    return lax.dot_general(a, b, (((1,), (1,)), ((), ())), preferred_element_type=f32)


def dot_nn(a, b):
    return lax.dot_general(a, b, (((1,), (0,)), ((), ())), preferred_element_type=f32)


def row_of(ref):
    return ref[...].reshape(1, ref.shape[0])


def down(row):
    return jnp.broadcast_to(row.astype(f32), (row.shape[1], row.shape[1])).T


def same(a, b):
    return (a == b).astype(f32)


def lanes_rows(rows):
    shape = (rows, STRETCH)
    return lax.broadcasted_iota(jnp.int32, shape, 1), lax.broadcasted_iota(jnp.int32, shape, 0)


def chain(ids, left_of, right_of, tails, blocks, out_ref, j):
    total = None
    for b in range(blocks):
        here = dot_nn(left_of(b, tails[b]), right_of(b))
        if b:
            here = here + same(ids[(b + 1) * STRETCH - 1], ids[b * STRETCH - 1]) * total
        total = here
        if b < blocks - 1:
            out_ref[j, b] = total
    return total


def gram_kernel(heads, ids, key_ref, gate_ref, segs_ref, packed_ref, grams_ref, wg_ref, wm_ref):
    tokens = key_ref.shape[0]
    blocks = tokens // STRETCH
    segs = row_of(segs_ref)
    spans = [slice(b * STRETCH, (b + 1) * STRETCH) for b in range(blocks)]
    tails = [same(segs[:, spans[b]], ids[(b + 1) * STRETCH - 1]) for b in range(blocks)]
    lane, row = lanes_rows(HALF)
    for j in range(STATE_HEADS):
        head = pl.program_id(0) * STATE_HEADS + j
        keys = key_ref[:, j * STRETCH:(j + 1) * STRETCH]
        keys_t = keys.astype(f32).T
        scale = lax.rsqrt(jnp.sum(keys_t * keys_t, axis=0, keepdims=True) + 1e-06)
        for_memory = gate_ref[pl.ds(head, 1), :] * scale
        for_gram = for_memory * scale
        wg_ref[pl.ds(head, 1), :] = for_gram
        wm_ref[pl.ds(head, 1), :] = for_memory
        gram = chain(
            ids,
            lambda b, tail: wide(keys_t[:, spans[b]] * (for_gram[:, spans[b]] * tail)),
            lambda b: twice(keys[spans[b]], 0),
            tails, blocks, grams_ref, j,
        )
        top, bottom = gram[:HALF], gram[HALF:]
        packed_ref[pl.ds(pl.multiple_of(head * HALF, HALF), HALF), :] = jnp.where(
            lane > row, top, pltpu.roll(bottom, HALF, 1)
        )
        packed_ref[pl.ds(heads * HALF + head, 1), :] = jnp.sum(
            jnp.where(lane == row, top, 0.0), axis=0, keepdims=True
        )

    @pl.when(pl.program_id(0) == 0)
    def _():
        rest = packed_ref.shape[0] - heads * HALF - heads
        packed_ref[pl.ds(heads * HALF + heads, rest), :] = jnp.full(
            (rest, STRETCH), ids[tokens - 1].astype(f32)
        )


def memory_kernel(ids, key_ref, value_ref, segs_ref, wm_ref, memory_ref, memories_ref):
    tokens = key_ref.shape[0]
    blocks = tokens // STRETCH
    segs = row_of(segs_ref)
    spans = [slice(b * STRETCH, (b + 1) * STRETCH) for b in range(blocks)]
    tails = [same(segs[:, spans[b]], ids[(b + 1) * STRETCH - 1]) for b in range(blocks)]
    for j in range(STATE_HEADS):
        head = pl.program_id(0) * STATE_HEADS + j
        columns = slice(j * STRETCH, (j + 1) * STRETCH)
        values_t = value_ref[:, columns].astype(f32).T
        for_memory = wm_ref[pl.ds(head, 1), :]
        memory_ref[j] = chain(
            ids,
            lambda b, tail: wide(values_t[:, spans[b]] * (for_memory[:, spans[b]] * tail)),
            lambda b: twice(key_ref[spans[b], columns], 0),
            tails, blocks, memories_ref, j,
        )


def unpacked(packed, corner):
    lane, row = lanes_rows(HALF)
    top = jnp.where(lane > row, packed, jnp.where(lane == row, 0.5 * corner, 0.0))
    low = jnp.where(lane < row, packed, jnp.where(lane == row, 0.5 * packed, 0.0))
    part = jnp.concatenate([top, pltpu.roll(low, HALF, 1)], axis=0)
    return part + part.T


def pair_kernel(tag, odd, local_ref, across_ref, pair_ref):
    is_odd = jnp.full((1, STRETCH), odd[0], jnp.int32) == 1
    local, across = local_ref[...], across_ref[...]
    equal = same(local_ref[tag:tag + 1, :], across_ref[tag:tag + 1, :])
    later = jnp.where(is_odd, local, across)
    earlier = jnp.where(is_odd, across, local)
    pair_ref[...] = later + equal * earlier
    pair_ref[tag:, :] = jnp.where(is_odd, local_ref[tag:, :], across_ref[tag:, :])


def pair_memory_kernel(heads, tag, odd, tag_ref, across_tag_ref, local_ref, across_ref, pair_ref):
    is_odd = jnp.full((1, STRETCH), odd[0], jnp.int32) == 1
    equal = same(tag_ref[tag:tag + 1, :], across_tag_ref[tag:tag + 1, :])
    of_local, of_across = jnp.where(is_odd, 1.0, equal), jnp.where(is_odd, equal, 1.0)
    for j in range(heads):
        pair_ref[j] = of_local * local_ref[j] + of_across * across_ref[j]


def normed(query):
    query = query.astype(f32)
    return query * lax.rsqrt(jnp.sum(query * query, axis=1, keepdims=True) + 1e-06)


def tables(ids, segs_ref, mask_ref, keep_ref):
    blocks = mask_ref.shape[0]

    @pl.when(pl.program_id(0) == 0)
    def _():
        segs = row_of(segs_ref)
        lane, row = lanes_rows(STRETCH)
        for b in range(blocks):
            here = segs[:, b * STRETCH:(b + 1) * STRETCH]
            below = down(here)
            mask_ref[b] = jnp.where((lane <= row) & (below == here.astype(f32)), 1.0, 0.0)
            keep_ref[b] = same(below, ids[max(b * STRETCH - 1, 0)].astype(f32))


def open_kernel(ids, ridge, query_ref, key_ref, segs_ref, wg_ref, grams_ref, image_ref, mask_ref, keep_ref):
    blocks = key_ref.shape[0] // STRETCH
    tables(ids, segs_ref, mask_ref, keep_ref)
    for j in range(SOLVE_HEADS):
        head = pl.program_id(0) * SOLVE_HEADS + j
        columns = slice(j * STRETCH, (j + 1) * STRETCH)
        for_gram = wg_ref[pl.ds(head, 1), :]
        for b in range(blocks):
            span = slice(b * STRETCH, (b + 1) * STRETCH)
            keys = key_ref[span, columns]
            query = normed(query_ref[span, columns])
            parts = wide(query)
            right = twice(keys.T, 0)
            image = ridge[head] * query
            if b:
                gram_high, gram_low = halves(grams_ref[j, b - 1])
                right = jnp.concatenate([right, twice(gram_high, 0), twice(gram_low, 0)], axis=1)
            found = dot_nn(parts, right)
            if b:
                image = image + (found[:, STRETCH:2 * STRETCH] + found[:, 2 * STRETCH:]) * keep_ref[b]
            weighed = found[:, :STRETCH] * (mask_ref[b] * for_gram[:, span])
            image_ref[span, columns] = image + dot_nn(wide(weighed), twice(keys, 0))


def solve_kernel(heads, ids, ridge, odd, query_ref, key_ref, value_ref, segs_ref, wg_ref, wm_ref, image_ref, across_ref, across_end_ref, above_ref, above_end_ref, next_ref, next_end_ref, pair_ref, pair_end_ref, grams_ref, memories_ref, solved_ref, partial_ref, mask_ref, keep_ref):
    blocks = key_ref.shape[0] // STRETCH
    every = [(j, b) for j in range(SOLVE_HEADS) for b in range(blocks)]
    spans = [slice(b * STRETCH, (b + 1) * STRETCH) for b in range(blocks)]
    columns = [slice(j * STRETCH, (j + 1) * STRETCH) for j in range(SOLVE_HEADS)]
    first_head = pl.program_id(0) * SOLVE_HEADS
    tables(ids, segs_ref, mask_ref, keep_ref)
    first = ids[0].astype(f32)
    arrived = [(across_ref, across_end_ref, odd[0].astype(f32)), (above_ref, above_end_ref, 1.0), (next_ref, next_end_ref, 1.0), (pair_ref, pair_end_ref, 1.0)]
    takes = [same(end[heads:heads + 1, :], first) * use for _, end, use in arrived]
    incoming = []
    for j in range(SOLVE_HEADS):
        here = slice(j * HALF, (j + 1) * HALF)
        at = pl.ds(first_head + j, 1)
        packed = corner = 0.0
        for take, (ref, end, _) in zip(takes, arrived):
            packed = packed + take * ref[here]
            corner = corner + take * end[at, :]
        incoming.append(unpacked(packed, corner))
    lam = [ridge[first_head + j] for j in range(SOLVE_HEADS)]
    for_gram = [wg_ref[pl.ds(first_head + j, 1), :] for j in range(SOLVE_HEADS)]
    for_memory = [wm_ref[pl.ds(first_head + j, 1), :] for j in range(SOLVE_HEADS)]
    joins = [same(ids[max(b * STRETCH - 1, 0)], ids[0]) for b in range(blocks)]
    twin, keys_t, right, weights = {}, {}, {}, {}
    direction, residual, solved, size_sq = {}, {}, {}, {}
    enter = []
    for j in range(SOLVE_HEADS):
        gram_high, gram_low = halves(incoming[j])
        enter.append(jnp.concatenate([twice(gram_high, 0), twice(gram_low, 0)], axis=1))
    query = {c: normed(query_ref[spans[c[1]], columns[c[0]]]) for c in every}
    found = {c: dot_nn(wide(query[c]), enter[c[0]]) for c in every}
    for c in every:
        j, b = c
        keys = key_ref[spans[b], columns[j]]
        twin[c] = twice(keys, 0)
        keys_t[c] = twice(keys.T, 0)
        weights[c] = mask_ref[b] * for_gram[j][:, spans[b]]
        if b:
            high, low = halves(grams_ref[j, b - 1] + joins[b] * incoming[j])
            right[c] = jnp.concatenate([twice(high, 0), twice(low, 0), keys_t[c]], axis=1)
        else:
            right[c] = jnp.concatenate([enter[j], keys_t[c]], axis=1)
    for c in every:
        j, b = c
        image = image_ref[spans[b], columns[j]] + (found[c][:, :STRETCH] + found[c][:, STRETCH:]) * (keep_ref[b] * joins[b])
        first_sq = jnp.sum(query[c] * query[c], axis=1, keepdims=True)
        step = first_sq / jnp.sum(query[c] * image, axis=1, keepdims=True)
        solved[c] = step * query[c]
        residual[c] = query[c] - step * image
        size_sq[c] = jnp.sum(residual[c] * residual[c], axis=1, keepdims=True)
        direction[c] = residual[c] + (size_sq[c] / first_sq) * query[c]
    for sweep in range(1, ITERS):
        found = {c: dot_nn(wide(direction[c]), right[c]) for c in every}
        for c in every:
            carried = (found[c][:, :STRETCH] + found[c][:, STRETCH:2 * STRETCH]) * keep_ref[c[1]] + lam[c[0]] * direction[c]
            scores = found[c][:, 2 * STRETCH:]
            weighed = scores * weights[c]
            if sweep < ITERS - 1:
                image = carried + dot_nn(wide(weighed), twin[c])
            step = size_sq[c] / jnp.sum(weighed * scores + carried * direction[c], axis=1, keepdims=True)
            solved[c] = solved[c] + step * direction[c]
            if sweep < ITERS - 1:
                residual[c] = residual[c] - step * image
                fresh_sq = jnp.sum(residual[c] * residual[c], axis=1, keepdims=True)
                direction[c] = residual[c] + (fresh_sq / size_sq[c]) * direction[c]
                size_sq[c] = fresh_sq
    parts = {c: wide(solved[c]) for c in every}
    scores = {c: dot_nn(parts[c], keys_t[c]) for c in every}
    found = {}
    for j, b in every:
        if b:
            high, low = halves(memories_ref[j, b - 1])
            found[j, b] = dot_nt(parts[j, b], jnp.concatenate([twice(high, 1), twice(low, 1)], axis=0))
    for j, b in every:
        c = j, b
        solved_ref[spans[b], columns[j]] = solved[c]
        weighed = scores[c] * (mask_ref[b] * for_memory[j][:, spans[b]])
        local = dot_nn(wide(weighed), twice(value_ref[spans[b], columns[j]], 0))
        if b:
            local = local + (found[c][:, :STRETCH] + found[c][:, STRETCH:]) * keep_ref[b]
        partial_ref[spans[b], columns[j]] = local


def read_kernel(heads, ids, odd, solved_ref, partial_ref, segs_ref, across_ref, across_end_ref, above_ref, above_end_ref, next_ref, next_end_ref, pair_ref, pair_end_ref, far_ref, out_ref):
    first = ids[0].astype(f32)
    segs = row_of(segs_ref)
    blocks = segs.shape[1] // STRETCH
    keep = jnp.concatenate([same(down(segs[:, b * STRETCH:(b + 1) * STRETCH]), first) for b in range(blocks)], axis=0)
    arrived = [(across_ref, across_end_ref, odd[0].astype(f32)), (above_ref, above_end_ref, 1.0), (next_ref, next_end_ref, 1.0), (pair_ref, pair_end_ref, 1.0), (far_ref, pair_end_ref, 1.0)]
    takes = [same(end[heads:heads + 1, :], first) * use for _, end, use in arrived]
    for j in range(READ_HEADS):
        columns = slice(j * STRETCH, (j + 1) * STRETCH)
        memory = 0.0
        for take, (ref, _, _) in zip(takes, arrived):
            memory = memory + take * ref[j]
        memory_high, memory_low = halves(memory)
        right = jnp.concatenate([twice(memory_high, 1), twice(memory_low, 1)], axis=0)
        found = dot_nt(wide(solved_ref[:, columns]), right)
        carried = (found[:, :STRETCH] + found[:, STRETCH:]) * keep
        out_ref[:, columns] = (partial_ref[:, columns] + carried).astype(out_ref.dtype)


def moved(block, source):
    count = lax.axis_size(AXES[0]) * lax.axis_size(AXES[1])
    route = [(source(i), i) for i in range(count) if source(i) is not None and 0 <= source(i) < count]
    return lax.ppermute(block, AXES, route)


def first_round(local):
    across = moved(local, lambda i: i ^ 1)
    above = moved(local, lambda i: i - 4)
    return across, above


def crosses(i):
    return i % 16 < 2


def paired(pair, wanted=lambda i: True):
    return moved(pair, lambda i: i - 1 - 2 * (i % 2) if wanted(i) else None)


def handed(above):
    return moved(above, lambda i: None if i % 2 else i + 1)


def body(queries, key_vectors, value_vectors, write_gate, ridge_term, segment_ids):
    tokens, width = queries.shape
    heads = ridge_term.shape[0]
    size = width // heads
    blocks = tokens // STRETCH
    smem = pl.BlockSpec(memory_space=pltpu.SMEM)
    ends = 16
    tag = heads * HALF + heads
    length = heads * HALF + ends

    def whole(*shape):
        return pl.BlockSpec(shape, lambda h: (0,) * len(shape))

    def column(n):
        return pl.BlockSpec((tokens, n * size), lambda h: (0, h))

    def state(n):
        return pl.BlockSpec((n, size, size), lambda h: (h, 0, 0))

    def inner(n):
        return pl.BlockSpec((n, blocks - 1, size, size), lambda h: (h, 0, 0, 0))

    def packed(n):
        return pl.BlockSpec((n * HALF, size), lambda h: (h, 0))

    end = pl.BlockSpec((ends, size), lambda h: (heads * HALF // ends, 0))
    rows = whole(heads, tokens)

    def grant(mebibytes):
        return pltpu.CompilerParams(vmem_limit_bytes=mebibytes * MIB)

    def shaped(*shape):
        return jax.ShapeDtypeStruct(shape, f32)

    def cost(flops, moved_bytes):
        return pl.CostEstimate(flops=flops, bytes_accessed=moved_bytes, transcendentals=0)

    gram, grams, for_gram, for_memory = pl.pallas_call(
        functools.partial(gram_kernel, heads),
        grid=(heads // STATE_HEADS,),
        in_specs=[smem, column(STATE_HEADS), rows, whole(tokens)],
        out_specs=[whole(length, size), inner(STATE_HEADS), rows, rows],
        out_shape=[shaped(length, size), shaped(heads, blocks - 1, size, size), shaped(heads, tokens), shaped(heads, tokens)],
        compiler_params=grant(56),
        name="grams",
    )(segment_ids, key_vectors, write_gate, segment_ids)
    across, above = first_round(gram)
    memory, memories = pl.pallas_call(
        memory_kernel,
        grid=(heads // STATE_HEADS,),
        in_specs=[smem, column(STATE_HEADS), column(STATE_HEADS), whole(tokens), rows],
        out_specs=[state(STATE_HEADS), inner(STATE_HEADS)],
        out_shape=[shaped(heads, size, size), shaped(heads, blocks - 1, size, size)],
        compiler_params=grant(56),
        cost_estimate=cost(10**9, 10**7),
        name="memories",
    )(segment_ids, key_vectors, value_vectors, segment_ids, for_memory)
    across_m, above_m = first_round(memory)

    odd = (lax.axis_index(AXES) % 2).astype(jnp.int32).reshape(1)
    vmem = pl.BlockSpec(memory_space=pltpu.VMEM)
    pair = pl.pallas_call(
        functools.partial(pair_kernel, tag),
        in_specs=[smem, vmem, vmem],
        out_specs=vmem,
        out_shape=shaped(length, size),
        compiler_params=grant(8),
        name="pair",
    )(odd, gram, across)
    pair, above, queries = lax.optimization_barrier((pair, above, queries))
    pair_in, next_in = paired(pair), handed(above)

    tables = [pltpu.VMEM((blocks, STRETCH, STRETCH), f32), pltpu.VMEM((blocks, STRETCH, STRETCH), f32)]
    image = pl.pallas_call(
        open_kernel,
        grid=(heads // SOLVE_HEADS,),
        in_specs=[smem, smem, column(SOLVE_HEADS), column(SOLVE_HEADS), whole(tokens), rows, inner(SOLVE_HEADS)],
        out_specs=column(SOLVE_HEADS),
        out_shape=shaped(tokens, width),
        scratch_shapes=tables,
        compiler_params=grant(28),
        cost_estimate=cost(4 * 10**9, 10**7),
        name="open",
    )(segment_ids, ridge_term, queries, key_vectors, segment_ids, for_gram, grams)

    pair_m = pl.pallas_call(
        functools.partial(pair_memory_kernel, heads, tag),
        in_specs=[smem, vmem, vmem, vmem, vmem],
        out_specs=vmem,
        out_shape=shaped(heads, size, size),
        compiler_params=grant(8),
        name="pair_memory",
    )(odd, gram, across, memory, across_m)
    pair_m, image = lax.optimization_barrier((pair_m, image))
    next_m_in = handed(above_m)
    near_m_in = paired(pair_m, lambda i: not crosses(i))
    pair_m, pair_in = lax.optimization_barrier((pair_m, pair_in))
    far_m_in = paired(pair_m, crosses)

    solved, partial = pl.pallas_call(
        functools.partial(solve_kernel, heads),
        grid=(heads // SOLVE_HEADS,),
        in_specs=[smem, smem, smem, column(SOLVE_HEADS), column(SOLVE_HEADS), column(SOLVE_HEADS), whole(tokens), rows, rows, column(SOLVE_HEADS)]
        + [packed(SOLVE_HEADS), end] * 4
        + [inner(SOLVE_HEADS), inner(SOLVE_HEADS)],
        out_specs=[column(SOLVE_HEADS), column(SOLVE_HEADS)],
        out_shape=[shaped(tokens, width), shaped(tokens, width)],
        scratch_shapes=tables,
        compiler_params=grant(20),
        cost_estimate=cost(2 * 10**10, 2 * 10**7),
        name="solve",
    )(
        segment_ids, ridge_term, odd, queries, key_vectors, value_vectors, segment_ids, for_gram, for_memory, image,
        across, across, above, above, next_in, next_in, pair_in, pair_in, grams, memories,
    )
    return pl.pallas_call(
        functools.partial(read_kernel, heads),
        grid=(heads // READ_HEADS,),
        in_specs=[smem, smem, column(READ_HEADS), column(READ_HEADS), whole(tokens)] + [state(READ_HEADS), end] * 4 + [state(READ_HEADS)],
        out_specs=column(READ_HEADS),
        out_shape=jax.ShapeDtypeStruct((tokens, width), jnp.bfloat16),
        compiler_params=grant(16),
        name="read",
    )(segment_ids, odd, solved, partial, segment_ids, across_m, across, above_m, above, next_m_in, next_in, near_m_in, pair_in, far_m_in)


def solution(mesh):
    return jax.shard_map(
        body,
        mesh=mesh,
        in_specs=(
            P(AXES, None),
            P(AXES, None),
            P(AXES, None),
            P(None, AXES),
            P(),
            P(AXES),
        ),
        out_specs=P(AXES, None),
        check_vma=False,
    )
```
